32 devices in a mesh: wa: 4 (over z), ha: 8 (over y, x, core).
Axes of the slice: x: 2, y: 2, z: 4, core: 2. Of those that a mesh axis runs over, the one named last changes fastest.
Arguments:
- tokens: bfloat16 [1024, 16384], P('ha', 'wa'), may hold values from -6 to 6
- gain_attn: bfloat16 [16384], P('wa'), may hold values from 0.25 to 1.75
- w_query: bfloat16 [16384, 16384], P('wa', 'ha'), may hold values from -0.046875 to 0.046875, as said below
- w_key: bfloat16 [16384, 1024], P('wa'), may hold values from -1.171875 to 1.171875, as said below
- w_value: bfloat16 [16384, 1024], P('wa'), may hold values from -0.046875 to 0.046875
- w_out: bfloat16 [16384, 16384], P('ha', 'wa'), may hold values from -0.1875 to 0.1875
- gain_ffn: bfloat16 [16384], P('wa'), may hold values from 0.25 to 1.75
- segment_ids: int32 [1024], replicated, may hold values from 0 to 31, never falling along the last dimension, each value on 1 to 256 neighbouring positions
Outputs:
- residual_out: bfloat16 [1024, 16384], P('ha', 'wa')
- ffn_input: bfloat16 [1024, 16384], P('ha', 'wa')
The draws below stay inside these ranges and needn't reach their ends.
Inputs may be any that keep to these rules, and one draw needn't show every extreme that they name: `w_query`: entries scaled by 16384 ** -0.5. `w_key`: entries scaled by 16384 ** -0.5. `segment_ids`: segment ids never fall along the tokens; each prompt has 1 to 256 tokens and one has exactly 256.
All inputs are finite; a program needn't handle non-finite values.
Results may differ from the reference program's by a relative error of at most 0.00675.
The reference program's roundings to bfloat16 on the way (of `scaled`, `queries`, `keys`, `weights` and `head_out`) count: a program that leaves them out, or rounds other values in their place, can miss the bound.
Values may be sent and summed in bfloat16 or wider, within the bound.
A program may use at most 192 MiB of HBM per device.

```python
import math
import jax
import jax.numpy as jnp
import numpy as np
from jax import lax

D = 16384
H = 128
KVH = 8
HD = 128
TOKENS = 1024
LMAX = 256


def query_base(key):
    noise = jax.random.normal(jax.random.fold_in(key, 11), (D, H * HD), jnp.float32)
    return jnp.clip(noise, -6.0, 6.0) * D ** (-0.5)


def draw_w_query(key, part):
    return query_base(key).astype(jnp.bfloat16)


def draw_w_key(key, part):
    noise = jax.random.normal(jax.random.fold_in(key, 23), (D, KVH * HD), jnp.float32)
    noise = jnp.clip(noise, -6.0, 6.0) * D ** (-0.5)
    return noise.astype(jnp.bfloat16)


def level_of(key, extent, cuts, smallest, high):
    def one(axis_at, blocks):
        draws = jax.random.uniform(jax.random.fold_in(jax.random.fold_in(key, 6), axis_at), (blocks,), jnp.float32, smallest / len(cuts), high / len(cuts))
        return jnp.repeat(jnp.exp(draws), extent[axis_at] // blocks).reshape((-1,) + (1,) * (len(extent) - axis_at - 1))

    gain = one(*cuts[0])
    for cut in cuts[1:]:
        gain = gain * one(*cut)
    return gain


def length_profile(amount, total, bound, lean):
    weights = [(1 << 20) // math.isqrt(rank ** lean) + 1 for rank in range(2, amount + 1)]
    rest, given = total - bound - (amount - 1), [1] * (amount - 1)
    while rest > 0:
        free = [i for i in range(amount - 1) if given[i] < bound]
        pool, budget = sum([weights[i] for i in free]), rest
        for i in free:
            addition = min(bound - given[i], max(1, budget * weights[i] // pool), rest)
            given[i] = given[i] + addition
            rest = rest - addition
    return np.array([bound] + given)


def ragged_sizes(rng, amount, total, most, skew):
    if amount == 2:
        one = jax.random.randint(rng, (), max(1, total - most), min(most, total - 1) + 1)
        return jnp.stack([one, total - one])
    sizes = jnp.asarray(length_profile(amount, total, most, skew), jnp.int32)
    twos = (amount - 1) // 2
    donor, taker = sizes[1:1 + 2 * twos:2], sizes[2:2 + 2 * twos:2]
    margin = jnp.minimum(donor - 1, most - taker)
    moved = jax.random.randint(jax.random.fold_in(rng, 1), (twos,), 0, 1 << 20) % (margin + 1)
    sizes = sizes.at[1:1 + 2 * twos:2].set(donor - moved).at[2:2 + 2 * twos:2].set(taker + moved)
    return sizes[jax.random.permutation(jax.random.fold_in(rng, 2), amount)]


def gaussian(stream_key, extent, deviation, limit, cuts=(), kind=jnp.bfloat16):
    factor_of = level_of(stream_key, extent, cuts, -0.22, 0.18) if cuts else 1.0
    drawn = jax.random.normal(stream_key, extent, jnp.float32) * deviation * factor_of
    return jnp.minimum(jnp.maximum(drawn, -limit), limit).astype(kind)


def setup_inputs(seed: int = 0) -> dict:
    key_list = jax.random.split(jax.random.key(seed), 9)
    return {
        "tokens": gaussian(key_list[0], (TOKENS, D), 1.0, 6.0, ((0, 8), (1, 4))),
        "gain_attn": jnp.clip(1.0 + 0.15 * jax.random.normal(key_list[1], (D,), jnp.float32), 0.25, 1.75).astype(jnp.bfloat16),
        "w_query": draw_w_query(jax.random.fold_in(key_list[8], 71), 0),
        "w_key": draw_w_key(jax.random.fold_in(key_list[8], 71), 0),
        "w_value": gaussian(key_list[4], (D, KVH * HD), D ** -0.5, 0.046875, ((0, 4),)),
        "w_out": gaussian(key_list[5], (H * HD, D), (H * HD // 16) ** -0.5, 0.1875, ((0, 8), (1, 4))),
        "gain_ffn": jnp.clip(1.0 + 0.15 * jax.random.normal(key_list[6], (D,), jnp.float32), 0.25, 1.75).astype(jnp.bfloat16),
        "segment_ids": jnp.searchsorted(jnp.cumsum(ragged_sizes(key_list[7], TOKENS // 32, TOKENS, LMAX, 2)), jnp.arange(TOKENS), side="right").astype(jnp.int32),
    }


EPS = 1e-05

def positions(segment_ids):
    index = jnp.arange(segment_ids.shape[0], dtype=jnp.int32)
    fresh = jnp.concatenate([jnp.ones((1,), dtype=bool), segment_ids[1:] != segment_ids[:-1]])
    start = lax.cummax(jnp.where(fresh, index, jnp.zeros_like(index)), axis=0)
    return (index - start).astype(jnp.float32)

def rope_tables(position):
    half = HD // 2
    inverse = 500000.0 ** (-(jnp.arange(half, dtype=jnp.float32) * 2.0 / HD))
    angle = position[:, None] * inverse[None, :]
    return (jnp.cos(angle), jnp.sin(angle))

def rotate(values, cosine, sine):
    half = values.shape[-1] // 2
    first = values[..., :half]
    second = values[..., half:]
    cosine = cosine[:, None, :]
    sine = sine[:, None, :]
    return jnp.concatenate([first * cosine - second * sine, second * cosine + first * sine], axis=-1)

def reference(tokens, gain_attn, w_query, w_key, w_value, w_out, gain_ffn, segment_ids):
    count = tokens.shape[0]
    token_f = tokens.astype(jnp.float32)
    row_scale = lax.rsqrt(lax.optimization_barrier(jnp.mean(token_f * token_f, axis=1)) + EPS)
    scaled = (token_f * gain_attn.astype(jnp.float32)).astype(jnp.bfloat16)
    cosine, sine = rope_tables(positions(segment_ids))
    query_f = jnp.dot(scaled, w_query, preferred_element_type=jnp.float32) * row_scale[:, None]
    queries = rotate(query_f.reshape(count, H, HD), cosine, sine).astype(jnp.bfloat16)
    key_plain = (jnp.dot(scaled, w_key, preferred_element_type=jnp.float32) * row_scale[:, None]).astype(jnp.bfloat16)
    key_plain = lax.optimization_barrier(key_plain)
    keys = rotate(key_plain.astype(jnp.float32).reshape(count, KVH, HD), cosine, sine).astype(jnp.bfloat16)
    values = (jnp.dot(scaled, w_value, preferred_element_type=jnp.float32) * row_scale[:, None]).astype(jnp.bfloat16)
    values = values.reshape(count, KVH, HD)
    index = jnp.arange(count, dtype=jnp.int32)
    allowed = (segment_ids[:, None] == segment_ids[None, :]) & (index[None, :] <= index[:, None])
    grouped = queries.reshape(count, KVH, H // KVH, HD).transpose(1, 0, 2, 3)

    def one_group(items):
        query_h, key_h, value_h = items
        scores = jnp.einsum('tgd,sd->gts', query_h.astype(jnp.float32), key_h.astype(jnp.float32)) * HD ** (-0.5)
        scores = jnp.where(allowed[None], scores, -1e+30)
        peak = lax.optimization_barrier(jnp.max(scores, axis=-1, keepdims=True))
        expo = jnp.where(allowed[None], jnp.exp(scores - peak), 0.0)
        weights = (expo / lax.optimization_barrier(jnp.sum(expo, axis=-1, keepdims=True))).astype(jnp.bfloat16)
        return jnp.einsum('gts,sd->tgd', weights.astype(jnp.float32), value_h.astype(jnp.float32)).astype(jnp.bfloat16)
    head_out = lax.map(one_group, (grouped, keys.transpose(1, 0, 2), values.transpose(1, 0, 2)))
    head_out = head_out.transpose(1, 0, 2, 3).reshape(count, H * HD)
    attended = jnp.dot(head_out, w_out, preferred_element_type=jnp.float32)
    residual_out = (token_f + attended).astype(jnp.bfloat16)
    residual_f = residual_out.astype(jnp.float32)
    scale_two = lax.rsqrt(lax.optimization_barrier(jnp.mean(residual_f * residual_f, axis=1)) + EPS)
    ffn_input = (residual_f * scale_two[:, None] * gain_ffn.astype(jnp.float32)).astype(jnp.bfloat16)
    return (residual_out, ffn_input)
```

```python
import functools

import jax
import jax.numpy as jnp
from jax import lax
from jax.experimental import pallas as pl
from jax.experimental.pallas import tpu as pltpu
from jax.sharding import PartitionSpec as P

KVH = 8
HD = 128
WINDOW = 256
EPS = 1e-05
TILE = 256
WIDE = 512
SKEW = 2
RING = 4
F32 = jnp.float32
BF16 = jnp.bfloat16


def rope_rows():
    half = HD // 2
    inverse = 500000.0 ** (-(jnp.arange(half, dtype=F32) * 2.0 / HD))
    angle = jnp.arange(WINDOW, dtype=F32)[:, None] * inverse[None, :]
    cosine, sine = jnp.cos(angle), jnp.sin(angle)
    return jnp.concatenate([cosine, cosine, -sine, sine], axis=1)


def mirror(a, m, size):
    total, bit = 0, 1
    while bit < size:
        total = total + lax.rem(lax.div(a, bit) + lax.div(m, bit), 2) * bit
        bit *= 2
    return total


def send_to(src, dst, sems, at, **peer):
    return pltpu.make_async_remote_copy(
        src_ref=src,
        dst_ref=dst,
        send_sem=sems.at[(0,) + at],
        recv_sem=sems.at[(1,) + at],
        device_id=peer,
        device_id_type=pl.DeviceIdType.MESH,
    )


def greet(n, chips, me, chip, core):
    barrier = pltpu.get_barrier_semaphore()

    def signal(**peer):
        pl.semaphore_signal(
            barrier, inc=1, device_id=peer, device_id_type=pl.DeviceIdType.MESH
        )

    for d in range(1, n):
        signal(wa=lax.rem(me + d, n))
    for m in range(1, chips):
        signal(ha=mirror(chip, jnp.int32(m), chips) * 2 + core)
    signal(ha=chip * 2 + 1 - core)
    pl.semaphore_wait(barrier, n + chips - 1)


def column(row):
    r = row.shape[1]
    a = lax.broadcasted_iota(jnp.int32, (r, r), 0)
    b = lax.broadcasted_iota(jnp.int32, (r, r), 1)
    return jnp.sum(jnp.where(a == b, jnp.broadcast_to(row, (r, r)), 0.0), axis=1, keepdims=True)


def lane_sums(block):
    ones = jnp.ones((8, block.shape[1]), F32)
    return lax.dot_general(
        ones, block, (((1,), (1,)), ((), ())), precision=lax.Precision.HIGHEST,
        preferred_element_type=F32,
    )


def fold_lanes(x):
    total = x[:, :128]
    for g in range(1, x.shape[1] // 128):
        total = total + x[:, g * 128 : (g + 1) * 128]
    return total


def allowed_mask(seg_row, rows):
    keys = seg_row.shape[1]
    q_seg = column(seg_row[:, keys - rows :])
    q_at = lax.broadcasted_iota(jnp.int32, (rows, keys), 0) + (keys - rows)
    k_at = lax.broadcasted_iota(jnp.int32, (rows, keys), 1)
    return (q_seg == seg_row) & (k_at <= q_at)


def front_kernel(
    n, chips, rows, tiles, per_head,
    tok_hbm, gain_ref, wq_hbm, wk_hbm, wv_hbm, seg_ref, rope_ref,
    qo, kvo, sqo, cso,
    tok, scaled, w, parts, qr, ql, kr, kl, sqp, sqs, lsq,
    wsem, tsem, same_sem, pair_sem, rsem, lsem, ssem,
):
    me, ha = lax.axis_index("wa"), lax.axis_index("ha")
    core, chip = lax.rem(ha, 2), lax.div(ha, 2)
    last = n - 1
    units = tiles + 1
    count = chips * units
    hrows = rows // 2
    own_at = pl.multiple_of(core * rows, rows)
    kv_at = pl.multiple_of(lax.div(ha, per_head) * HD, HD)

    def w_copies(u):
        if u == 0:
            return [
                pltpu.make_async_copy(
                    wk_hbm.at[:, pl.ds(kv_at, HD)], w.at[0, :, pl.ds(0, HD)], wsem.at[0]
                ),
                pltpu.make_async_copy(
                    wv_hbm.at[:, pl.ds(kv_at, HD)], w.at[0, :, pl.ds(HD, HD)], wsem.at[1]
                ),
            ]
        return [
            pltpu.make_async_copy(
                wq_hbm.at[:, pl.ds((u - 1) * TILE, TILE)], w.at[u], wsem.at[u + 1]
            )
        ]

    own_copy = pltpu.make_async_copy(tok_hbm, tok.at[0, pl.ds(own_at, rows)], tsem)
    own_copy.start()
    for u in range(units):
        for copy in w_copies(u):
            copy.start()
    greet(n, chips, me, chip, core)

    def half_rows(f):
        return pl.ds(pl.multiple_of(own_at + f * hrows, hrows), hrows)

    def same_copy(m, f):
        return send_to(
            tok_hbm.at[pl.ds(f * hrows, hrows)], tok.at[m, half_rows(f)], same_sem, (m, f),
            ha=mirror(chip, m, chips) * 2 + core,
        )

    def pair_copy(m, f, first):
        src = tok_hbm.at[pl.ds(f * hrows, hrows)] if first else tok.at[m, half_rows(f)]
        return send_to(
            src, tok.at[m, half_rows(f)], pair_sem, (m, f), ha=chip * 2 + 1 - core
        )

    for f in range(2):
        pair_copy(jnp.int32(0), f, True).start()
    for m in range(1, min(3, chips)):
        for f in range(2):
            same_copy(jnp.int32(m), f).start()

    small = [
        send_to(sqs, lsq.at[d - 1], ssem, (d - 1,), wa=lax.rem(me + d, n)) for d in range(1, n)
    ]

    def prepare(m):
        there = mirror(chip, m, chips)

        @pl.loop(0, 2 * rows // 16)
        def _(g):
            at = pl.ds(pl.multiple_of(g * 16, 16), 16)
            x = tok[m, at, :].astype(F32)
            scaled[at, :] = (x * gain_ref[...].astype(F32)).astype(BF16)
            sqp[at, :] = fold_lanes(x * x)

        for e in range(2):
            sqs[pl.ds(there * 2 + e, 1), :] = lane_sums(sqp[pl.ds(e * rows, rows), :])[:1]

    def tables(m):
        for e in range(2):
            h = mirror(chip, m, chips) * 2 + e
            allowed = allowed_mask(seg_ref[h], rows)
            at = jnp.sum(jnp.where(allowed, 1.0, 0.0), axis=1, keepdims=True) - 1.0
            lanes = lax.broadcasted_iota(jnp.int32, (rows, WINDOW), 1)
            pick = jnp.where(lanes == at.astype(jnp.int32), 1.0, 0.0)
            cso[h] = jnp.dot(
                pick, rope_ref[...], precision=lax.Precision.HIGHEST,
                preferred_element_type=F32,
            )

    def handle(pos, peer, part, land, out, sems, j):
        first = send_to(part, land, sems, (j,), wa=peer)
        later = send_to(land, land, sems, (j,), wa=peer)

        @pl.when(pos == 0)
        def _():
            first.start()

        @pl.when(pos > 0)
        def _():
            later.wait_recv()

        @pl.when((pos > 0) & (pos < last))
        def _():
            land[...] = land[...] + part[...]
            later.start()

        @pl.when(pos == last)
        def _():
            out[...] = land[...] + part[...]

    def reduce_step(s, pos, peer, e, q_land, k_land, sems):
        j = s - SKEW * pos

        @pl.when((j >= 0) & (j < count))
        def _():
            m, u = lax.div(j, units), lax.rem(j, units)

            @pl.when(u == 0)
            def _():
                handle(pos, peer, parts.at[j], k_land.at[m], kvo.at[m], sems, j)

            @pl.when(u > 0)
            def _():
                jq = m * tiles + u - 1
                part = parts.at[j, pl.ds(e * rows, rows)]
                handle(pos, peer, part, q_land.at[jq], qo.at[jq], sems, j)

    right, left = jnp.minimum(me + 1, last), jnp.maximum(me - 1, 0)

    @pl.loop(0, count + SKEW * last)
    def _(s):
        m, u = lax.div(s, units), lax.rem(s, units)

        @pl.when(s < count)
        def _():
            @pl.when(u == 0)
            def _():
                @pl.when(m == 0)
                def _():
                    own_copy.wait()

                for f in range(2):
                    pair_copy(m, f, False).wait_recv()
                prepare(m)

                @pl.when(m == chips - 1)
                def _():
                    for copy in small:
                        copy.start()

            for v in range(units):

                @pl.when(s == v)
                def _():
                    for copy in w_copies(v):
                        copy.wait()

            parts[s] = jnp.dot(scaled[...], w[u], preferred_element_type=F32)

        reduce_step(s, me, right, 1, qr, kr, rsem)
        reduce_step(s, last - me, left, 0, ql, kl, lsem)

        @pl.when((s < count) & (u == 1))
        def _():
            tables(m)

        for f in range(2):
            turn = max(0, units - 4) if f == 0 else units - 1

            @pl.when((u == turn) & (m + 1 < chips))
            def _():
                same_copy(m + 1, f).wait_recv()
                pair_copy(m + 1, f, False).start()

            @pl.when((u == turn) & (m + 3 < chips))
            def _():
                same_copy(m + 3, f).start()

    def drain(j, pos, peer, e, q_land, k_land, sems):
        m, u = lax.div(j, units), lax.rem(j, units)

        @pl.when((pos < last) & (u == 0))
        def _():
            send_to(k_land.at[m], k_land.at[m], sems, (j,), wa=peer).wait_send()

        @pl.when((pos < last) & (u > 0))
        def _():
            jq = m * tiles + u - 1
            send_to(q_land.at[jq], q_land.at[jq], sems, (j,), wa=peer).wait_send()

    @pl.loop(0, count)
    def _(j):
        drain(j, me, right, 1, qr, kr, rsem)
        drain(j, last - me, left, 0, ql, kl, lsem)

    for m in range(chips):
        for f in range(2):
            pair_copy(jnp.int32(m), f, False).wait_send()
            if m:
                same_copy(jnp.int32(m), f).wait_send()
    for copy in small:
        copy.wait()
    total = sqs[...]
    for d in range(n - 1):
        total = total + lsq[d]
    sqo[...] = total


def front(tokens, gain, w_query, w_key, w_value, seg_rows, rope, n, n_ha):
    rows, width = tokens.shape
    cols = w_query.shape[1]
    chips, tiles = n_ha // 2, cols // TILE
    units = tiles + 1
    count = chips * units
    vmem, any_ = pl.BlockSpec(memory_space=pltpu.VMEM), pl.BlockSpec(memory_space=pl.ANY)
    dma = pltpu.SemaphoreType.DMA
    return pl.pallas_call(
        functools.partial(front_kernel, n, chips, rows, tiles, n_ha // KVH),
        out_shape=(
            jax.ShapeDtypeStruct((chips * tiles, rows, TILE), F32),
            jax.ShapeDtypeStruct((chips, 2 * rows, TILE), F32),
            jax.ShapeDtypeStruct((n_ha, rows), F32),
            jax.ShapeDtypeStruct((n_ha, rows, 2 * HD), F32),
        ),
        in_specs=[any_, vmem, any_, any_, any_, vmem, vmem],
        out_specs=(vmem,) * 4,
        scratch_shapes=[
            pltpu.VMEM((chips, 2 * rows, width), BF16),
            pltpu.VMEM((2 * rows, width), BF16),
            pltpu.VMEM((units, width, TILE), BF16),
            pltpu.VMEM((count, 2 * rows, TILE), F32),
            pltpu.VMEM((chips * tiles, rows, TILE), F32),
            pltpu.VMEM((chips * tiles, rows, TILE), F32),
            pltpu.VMEM((chips, 2 * rows, TILE), F32),
            pltpu.VMEM((chips, 2 * rows, TILE), F32),
            pltpu.VMEM((2 * rows, 128), F32),
            pltpu.VMEM((n_ha, rows), F32),
            pltpu.VMEM((n - 1, n_ha, rows), F32),
            dma((units + 1,)),
            dma,
            dma((2, chips, 2)),
            dma((2, chips, 2)),
            dma((2, count)),
            dma((2, count)),
            dma((2, n - 1)),
        ],
        compiler_params=pltpu.CompilerParams(
            collective_id=0, has_side_effects=True, vmem_limit_bytes=60 << 20
        ),
    )(tokens, gain, w_query, w_key, w_value, seg_rows, rope)


def back_kernel(
    n, chips, rows, tiles, wides, all_width,
    q_ref, kv_ref, sq_ref, cs_ref, seg_ref, tok_ref, gain_ref, wo_hbm,
    res_ref, ffn_ref,
    wo, keys, values, mask, head, acc, got, stage, land, own, sqp, sq2, lsq2,
    wsem, rsem, lsem, psem, xsem, ssem,
):
    me, ha = lax.axis_index("wa"), lax.axis_index("ha")
    core, chip = lax.rem(ha, 2), lax.div(ha, 2)
    last = n - 1
    n_chunk, n_unit = chips * tiles, chips * wides
    lag = tiles + SKEW * last
    window = WINDOW + rows
    end_row = jnp.where(me == last, 1, 0)
    partner = chip * 2 + 1 - core
    mine = pl.ds(pl.multiple_of(core * rows, rows), rows)
    theirs = pl.ds(pl.multiple_of((1 - core) * rows, rows), rows)

    def w_copy(k):
        return pltpu.make_async_copy(wo_hbm.at[:, pl.ds(k * WIDE, WIDE)], wo.at[k], wsem.at[k])

    for k in range(wides):
        w_copy(k).start()
    greet(n, chips, me, chip, core)

    def row_scale(h):
        return column(lax.rsqrt(sq_ref[pl.ds(h, 1), :] / all_width + EPS))

    def rotated(x, h):
        return x * cs_ref[h, :, :HD] + pltpu.roll(x, HD // 2, 1) * cs_ref[h, :, HD:]

    is_end = (me == 0) | (me == last)

    @pl.when(is_end)
    def _():
        zero = jnp.zeros((WINDOW, HD), BF16)
        keys[pl.ds(0, WINDOW), :] = zero
        values[pl.ds(0, WINDOW), :] = zero

        @pl.loop(0, chips)
        def _(m):
            there = mirror(chip, m, chips)
            for e in range(2):
                h = there * 2 + e
                at = pl.ds(pl.multiple_of(WINDOW + h * rows, rows), rows)
                scale = row_scale(h)
                block = kv_ref.at[m, pl.ds(e * rows, rows)]
                plain = (block[:, :HD] * scale).astype(BF16).astype(F32)
                keys[at, :] = rotated(plain, h).astype(BF16)
                values[at, :] = (block[:, HD:] * scale).astype(BF16)

    def attend(j):
        p, t = lax.div(j, tiles), lax.rem(j, tiles)
        m = chips - 1 - p
        h = mirror(chip, m, chips) * 2 + end_row

        @pl.when(t == 0)
        def _():
            mask[...] = jnp.where(allowed_mask(seg_ref[h], rows), 1.0, 0.0)

        at = pl.ds(pl.multiple_of(h * rows, rows), window)
        scale = row_scale(h)
        allowed = mask[...] > 0.5
        to = pl.ds(pl.multiple_of(end_row * rows, rows), rows)
        for x in range(TILE // HD):
            query = rotated(q_ref[m * tiles + t, :, x * HD : (x + 1) * HD] * scale, h).astype(BF16)
            scores = lax.dot_general(
                query, keys[at, :], (((1,), (1,)), ((), ())), preferred_element_type=F32
            ) * HD ** (-0.5)
            scores = jnp.where(allowed, scores, -1e30)
            peak = jnp.max(scores, axis=1, keepdims=True)
            expo = jnp.where(allowed, jnp.exp(scores - peak), 0.0)
            weights = (expo / jnp.sum(expo, axis=1, keepdims=True)).astype(BF16)
            out = jnp.dot(weights, values[at, :], preferred_element_type=F32)
            head[p, t, to, x * HD : (x + 1) * HD] = out.astype(BF16)

    def spread_copy(j, e, peer, sems):
        ref = head.at[lax.div(j, tiles), lax.rem(j, tiles), pl.ds(e * rows, rows)]
        return send_to(ref, ref, sems, (j,), wa=peer)

    def spread_step(s, pos, peer, e, sems):
        j = s - SKEW * pos

        @pl.when((j >= 0) & (j < n_chunk))
        def _():
            copy = spread_copy(j, e, peer, sems)

            @pl.when(pos > 0)
            def _():
                copy.wait_recv()

            @pl.when(pos < last)
            def _():
                copy.start()

    def pair_copy(v):
        return send_to(acc.at[lax.rem(v, RING), theirs], got.at[v], psem, (v,), ha=partner)

    def peer_copy(v):
        m = chips - 1 - lax.div(v, wides)
        return send_to(
            stage.at[v], land.at[v], xsem, (v,), ha=mirror(chip, m, chips) * 2 + core
        )

    def project(v):
        p, k = lax.div(v, wides), lax.rem(v, wides)
        for i in range(wides):

            @pl.when(v == i)
            def _():
                w_copy(i).wait()

        @pl.when(v >= RING)
        def _():
            pair_copy(v - RING).wait_send()

        block = jnp.concatenate([head[p, t] for t in range(tiles)], axis=1)
        for y in range(WIDE // TILE):
            at = slice(y * TILE, (y + 1) * TILE)
            acc[lax.rem(v, RING), :, at] = jnp.dot(
                block, wo[k, :, at], preferred_element_type=F32
            )
        pair_copy(v).start()

    def combine(v):
        p, k = lax.div(v, wides), lax.rem(v, wides)
        pair_copy(v).wait_recv()
        both = acc[lax.rem(v, RING), mine, :] + got[v]

        @pl.when(p < chips - 1)
        def _():
            stage[v] = both.astype(BF16)
            peer_copy(v).start()

        @pl.when(p == chips - 1)
        def _():
            own[k] = both

    right, left = jnp.minimum(me + 1, last), jnp.maximum(me - 1, 0)

    @pl.loop(0, n_unit + lag + 1)
    def _(s):
        @pl.when(is_end & (s < n_chunk))
        def _():
            attend(s)

        spread_step(s, me, right, 0, rsem)
        spread_step(s, last - me, left, 1, lsem)

        v = s - lag

        @pl.when((v >= 0) & (v < n_unit))
        def _():
            project(v)

        @pl.when(v >= 1)
        def _():
            combine(v - 1)

    @pl.loop(0, wides)
    def _(k):
        total = own[k]
        for p in range(chips - 1):
            peer_copy(p * wides + k).wait_recv()
            total = total + land[p * wides + k].astype(F32)
        at = pl.ds(pl.multiple_of(k * WIDE, WIDE), WIDE)
        res = (tok_ref[:, at].astype(F32) + total).astype(BF16)
        res_ref[:, at] = res
        wide = res.astype(F32)
        square = fold_lanes(wide * wide)

        @pl.when(k == 0)
        def _():
            sqp[...] = square

        @pl.when(k > 0)
        def _():
            sqp[...] = sqp[...] + square

    sq2[...] = lane_sums(sqp[...])
    small = [
        send_to(sq2, lsq2.at[d - 1], ssem, (d - 1,), wa=lax.rem(me + d, n)) for d in range(1, n)
    ]
    for copy in small:
        copy.start()

    @pl.loop(0, n_chunk)
    def _(j):
        @pl.when(me < last)
        def _():
            spread_copy(j, 0, right, rsem).wait_send()

        @pl.when(me > 0)
        def _():
            spread_copy(j, 1, left, lsem).wait_send()

    @pl.loop(0, n_unit - wides)
    def _(v):
        peer_copy(v).wait_send()

    for v in range(n_unit - RING, n_unit):
        pair_copy(jnp.int32(v)).wait_send()
    for copy in small:
        copy.wait()
    total = sq2[...]
    for d in range(n - 1):
        total = total + lsq2[d]
    scale_two = column(lax.rsqrt(total[:1] / all_width + EPS))

    @pl.loop(0, wides)
    def _(k):
        at = pl.ds(pl.multiple_of(k * WIDE, WIDE), WIDE)
        wide = res_ref[:, at].astype(F32)
        ffn_ref[:, at] = (wide * scale_two * gain_ref[:, at].astype(F32)).astype(BF16)


def back(q_sum, kv_sum, sq_sum, cs, seg_rows, tokens, gain, w_out, n, n_ha):
    rows, width = tokens.shape
    cols = w_out.shape[0]
    chips, tiles, wides = n_ha // 2, cols // TILE, width // WIDE
    n_chunk, n_unit = chips * tiles, chips * wides
    vmem, any_ = pl.BlockSpec(memory_space=pltpu.VMEM), pl.BlockSpec(memory_space=pl.ANY)
    dma = pltpu.SemaphoreType.DMA
    out = jax.ShapeDtypeStruct((rows, width), BF16)
    return pl.pallas_call(
        functools.partial(back_kernel, n, chips, rows, tiles, wides, width * n),
        out_shape=(out, out),
        in_specs=[vmem] * 7 + [any_],
        out_specs=(vmem, vmem),
        scratch_shapes=[
            pltpu.VMEM((wides, cols, WIDE), BF16),
            pltpu.VMEM((WINDOW + n_ha * rows, HD), BF16),
            pltpu.VMEM((WINDOW + n_ha * rows, HD), BF16),
            pltpu.VMEM((rows, WINDOW + rows), F32),
            pltpu.VMEM((chips, tiles, 2 * rows, TILE), BF16),
            pltpu.VMEM((RING, 2 * rows, WIDE), F32),
            pltpu.VMEM((n_unit, rows, WIDE), F32),
            pltpu.VMEM((n_unit - wides, rows, WIDE), BF16),
            pltpu.VMEM((n_unit - wides, rows, WIDE), BF16),
            pltpu.VMEM((wides, rows, WIDE), F32),
            pltpu.VMEM((rows, 128), F32),
            pltpu.VMEM((8, rows), F32),
            pltpu.VMEM((n - 1, 8, rows), F32),
            dma((wides,)),
            dma((2, n_chunk)),
            dma((2, n_chunk)),
            dma((2, n_unit)),
            dma((2, n_unit - wides)),
            dma((2, n - 1)),
        ],
        compiler_params=pltpu.CompilerParams(
            collective_id=1, has_side_effects=True, vmem_limit_bytes=60 << 20
        ),
    )(q_sum, kv_sum, sq_sum, cs, seg_rows, tokens, gain, w_out)


def on_device(tokens, gain_attn, w_query, w_key, w_value, w_out, gain_ffn, segment_ids):
    rows, width = tokens.shape
    n_wa = lax.axis_size("wa")
    n_ha = lax.axis_size("ha")
    padded = jnp.pad(segment_ids, (WINDOW, 0), constant_values=-1).astype(F32)
    seg_rows = jnp.stack([padded[None, h * rows : (h + 1) * rows + WINDOW] for h in range(n_ha)])
    q_sum, kv_sum, sq_sum, cs = front(
        tokens, gain_attn.reshape(1, width), w_query, w_key, w_value, seg_rows, rope_rows(),
        n_wa, n_ha,
    )
    return back(
        q_sum, kv_sum, sq_sum, cs, seg_rows, tokens, gain_ffn.reshape(1, width), w_out,
        n_wa, n_ha,
    )


def solution(mesh):
    in_specs = (
        P("ha", "wa"),
        P("wa"),
        P("wa", "ha"),
        P("wa", None),
        P("wa", None),
        P("ha", "wa"),
        P("wa"),
        P(),
    )
    out_specs = (P("ha", "wa"), P("ha", "wa"))
    return jax.shard_map(
        on_device, mesh=mesh, in_specs=in_specs, out_specs=out_specs, check_vma=False
    )
```

```python
import functools

import jax
import jax.numpy as jnp
from jax import lax
from jax.experimental import pallas as pl
from jax.experimental.pallas import tpu as pltpu
from jax.sharding import PartitionSpec as P

KVH = 8
HD = 128
WINDOW = 256
EPS = 1e-05
TILE = 256
WIDE = 512
SKEW = 3
LEVELS = 32766.0
FORWARD = 2
RING = 4
F32 = jnp.float32
BF16 = jnp.bfloat16


def rope_rows():
    half = HD // 2
    inverse = 500000.0 ** (-(jnp.arange(half, dtype=F32) * 2.0 / HD))
    angle = jnp.arange(WINDOW, dtype=F32)[:, None] * inverse[None, :]
    cosine, sine = jnp.cos(angle), jnp.sin(angle)
    return jnp.concatenate([cosine, cosine, -sine, sine], axis=1)


def mirror(a, m, size):
    total, bit = 0, 1
    while bit < size:
        total = total + lax.rem(lax.div(a, bit) + lax.div(m, bit), 2) * bit
        bit *= 2
    return total


def member(g, sub, chips):
    edge = (g == 0) | (g == chips - 1)
    low = lax.div(g - 1, 2) * 2 + 1
    return jnp.where(edge, g, low + sub), jnp.where(edge, sub, lax.rem(g - 1, 2))


def place(m, f, chips):
    edge = (m == 0) | (m == chips - 1)
    low = lax.div(m - 1, 2) * 2 + 1
    return jnp.where(edge, m, low + f), jnp.where(edge, f, lax.rem(m - 1, 2))


def send_to(src, dst, sems, at, **peer):
    return pltpu.make_async_remote_copy(
        src_ref=src,
        dst_ref=dst,
        send_sem=sems.at[(0,) + at],
        recv_sem=sems.at[(1,) + at],
        device_id=peer,
        device_id_type=pl.DeviceIdType.MESH,
    )


def greet(n, chips, me, chip, core):
    barrier = pltpu.get_barrier_semaphore()

    def signal(**peer):
        pl.semaphore_signal(
            barrier, inc=1, device_id=peer, device_id_type=pl.DeviceIdType.MESH
        )

    for d in range(1, n):
        signal(wa=lax.rem(me + d, n))
    for m in range(1, chips):
        signal(ha=mirror(chip, jnp.int32(m), chips) * 2 + core)
    signal(ha=chip * 2 + 1 - core)
    pl.semaphore_wait(barrier, n + chips - 1)


def column(row):
    r = row.shape[1]
    a = lax.broadcasted_iota(jnp.int32, (r, r), 0)
    b = lax.broadcasted_iota(jnp.int32, (r, r), 1)
    return jnp.sum(jnp.where(a == b, jnp.broadcast_to(row, (r, r)), 0.0), axis=1, keepdims=True)


def as_row(col):
    r = col.shape[0]
    a = lax.broadcasted_iota(jnp.int32, (r, r), 0)
    b = lax.broadcasted_iota(jnp.int32, (r, r), 1)
    return jnp.sum(jnp.where(a == b, jnp.broadcast_to(col, (r, r)), 0.0), axis=0, keepdims=True)


def encode(x, code, steps, rows):
    for i in range(x.shape[0] // rows):
        for y in range(TILE // HD):
            part = x[i * rows : (i + 1) * rows, y * HD : (y + 1) * HD]
            top = jnp.maximum(jnp.max(jnp.abs(part), axis=1, keepdims=True), 1e-30)
            whole = jnp.round(part * (LEVELS / top)).astype(jnp.int32)
            code[i * rows : (i + 1) * rows, y * HD : (y + 1) * HD] = whole.astype(jnp.int16)
            k = i * 2 + y
            steps[k : k + 1, :] = as_row(top * (1.0 / LEVELS))


def decode(code, steps, rows):
    blocks = []
    for i in range(code.shape[0] // rows):
        line = []
        for y in range(TILE // HD):
            part = code[i * rows : (i + 1) * rows, y * HD : (y + 1) * HD]
            k = i * 2 + y
            line.append(part.astype(jnp.int32).astype(F32) * column(steps[k : k + 1, :]))
        blocks.append(jnp.concatenate(line, axis=1))
    return jnp.concatenate(blocks, axis=0)


def lane_sums(block):
    ones = jnp.ones((8, block.shape[1]), F32)
    return lax.dot_general(
        ones, block, (((1,), (1,)), ((), ())), precision=lax.Precision.HIGHEST,
        preferred_element_type=F32,
    )


def fold_lanes(x):
    total = x[:, :128]
    for g in range(1, x.shape[1] // 128):
        total = total + x[:, g * 128 : (g + 1) * 128]
    return total


def allowed_mask(seg_row, rows):
    keys = seg_row.shape[1]
    q_seg = column(seg_row[:, keys - rows :])
    q_at = lax.broadcasted_iota(jnp.int32, (rows, keys), 0) + (keys - rows)
    k_at = lax.broadcasted_iota(jnp.int32, (rows, keys), 1)
    return (q_seg == seg_row) & (k_at <= q_at)


def front_kernel(
    n, chips, rows, tiles, per_head,
    tok_hbm, gain_ref, wq_hbm, wk_hbm, wv_hbm, seg_ref, rope_ref,
    qo, kvo, sqo, cso,
    tok, scaled, w, parts, qr, ql, kr, kl, er, el, sqp, sqs, lsq,
    wsem, tsem, same_sem, pair_sem, rsem, lsem, resem, lesem, ssem,
):
    me, ha = lax.axis_index("wa"), lax.axis_index("ha")
    core, chip = lax.rem(ha, 2), lax.div(ha, 2)
    last = n - 1
    units = tiles + 1
    count = chips * units
    hrows = rows // 2
    own_at = pl.multiple_of(core * rows, rows)
    kv_at = pl.multiple_of(lax.div(ha, per_head) * HD, HD)

    def w_copies(u):
        if u == 0:
            return [
                pltpu.make_async_copy(
                    wk_hbm.at[:, pl.ds(kv_at, HD)], w.at[0, :, pl.ds(0, HD)], wsem.at[0]
                ),
                pltpu.make_async_copy(
                    wv_hbm.at[:, pl.ds(kv_at, HD)], w.at[0, :, pl.ds(HD, HD)], wsem.at[1]
                ),
            ]
        return [
            pltpu.make_async_copy(
                wq_hbm.at[:, pl.ds((u - 1) * TILE, TILE)], w.at[u], wsem.at[u + 1]
            )
        ]

    own_copy = pltpu.make_async_copy(tok_hbm, tok.at[0, pl.ds(own_at, rows)], tsem)
    own_copy.start()
    for u in range(units):
        for copy in w_copies(u):
            copy.start()
    greet(n, chips, me, chip, core)

    def half_rows(f):
        return pl.ds(pl.multiple_of(f * hrows, hrows), hrows)

    def spot(m, f):
        g, part = place(m, f, chips)
        return tok.at[g, pl.ds(pl.multiple_of(own_at + part * hrows, hrows), hrows)]

    def same_copy(m, f):
        return send_to(
            tok_hbm.at[half_rows(f)], spot(m, f), same_sem, (m, f),
            ha=mirror(chip, m, chips) * 2 + core,
        )

    def pair_copy(m, f, first):
        src = tok_hbm.at[half_rows(f)] if first else spot(m, f)
        return send_to(src, spot(m, f), pair_sem, (m, f), ha=chip * 2 + 1 - core)

    for f in range(2):
        pair_copy(jnp.int32(0), f, True).start()
    for f in range(2):
        for m in range(1, min(3, chips)):
            same_copy(jnp.int32(m), f).start()

    small = [
        send_to(sqs, lsq.at[d - 1], ssem, (d - 1,), wa=lax.rem(me + d, n)) for d in range(1, n)
    ]

    def prepare(g):
        @pl.loop(0, 2 * rows // 16)
        def _(i):
            at = pl.ds(pl.multiple_of(i * 16, 16), 16)
            x = tok[g, at, :].astype(F32)
            scaled[at, :] = (x * gain_ref[...].astype(F32)).astype(BF16)
            sqp[at, :] = fold_lanes(x * x)

        for e in range(2):
            sqs[pl.ds(g * 2 + e, 1), :] = lane_sums(sqp[pl.ds(e * rows, rows), :])[:1]

    def tables(g):
        for e in range(2):
            for part in range(2):
                m, f = member(g, part, chips)
                allowed = allowed_mask(seg_ref[(mirror(chip, m, chips) * 2 + e) * 2 + f], hrows)
                at = jnp.sum(jnp.where(allowed, 1.0, 0.0), axis=1, keepdims=True) - 1.0
                lanes = lax.broadcasted_iota(jnp.int32, (hrows, WINDOW), 1)
                pick = jnp.where(lanes == at.astype(jnp.int32), 1.0, 0.0)
                cso[g * 2 + e, part * hrows : (part + 1) * hrows, :] = jnp.dot(
                    pick, rope_ref[...], precision=lax.Precision.HIGHEST,
                    preferred_element_type=F32,
                )

    def code_copies(land, steps, sems, step_sems, j, peer):
        return (
            send_to(land, land, sems, (j,), wa=peer),
            send_to(steps, steps, step_sems, (j,), wa=peer),
        )

    def handle(pos, peer, part, land, steps, out, sems, step_sems, j):
        copies = code_copies(land, steps, sems, step_sems, j, peer)

        @pl.when(pos == 0)
        def _():
            encode(part[...], land, steps, rows)

        @pl.when(pos > 0)
        def _():
            for copy in copies:
                copy.wait_recv()

        @pl.when((pos > 0) & (pos < last))
        def _():
            encode(decode(land, steps, rows) + part[...], land, steps, rows)

        @pl.when(pos < last)
        def _():
            for copy in copies:
                copy.start()

        @pl.when(pos == last)
        def _():
            out[...] = decode(land, steps, rows) + part[...]

    def reduce_step(s, pos, peer, e, q_land, k_land, steps, sems, step_sems):
        j = s - SKEW * pos

        @pl.when((j >= 0) & (j < count))
        def _():
            m, u = lax.div(j, units), lax.rem(j, units)

            @pl.when(u == 0)
            def _():
                handle(
                    pos, peer, parts.at[j], k_land.at[m], steps.at[j], kvo.at[m],
                    sems, step_sems, j,
                )

            @pl.when(u > 0)
            def _():
                jq = m * tiles + u - 1
                part = parts.at[j, pl.ds(e * rows, rows)]
                handle(
                    pos, peer, part, q_land.at[jq], steps.at[j], qo.at[jq],
                    sems, step_sems, j,
                )

    right, left = jnp.minimum(me + 1, last), jnp.maximum(me - 1, 0)

    @pl.loop(0, count + SKEW * last)
    def _(s):
        g, u = lax.div(s, units), lax.rem(s, units)

        @pl.when(s < count)
        def _():
            @pl.when(u == 0)
            def _():
                @pl.when(g == 0)
                def _():
                    own_copy.wait()

                for part in range(2):
                    pair_copy(*member(g, part, chips), False).wait_recv()
                prepare(g)

                @pl.when(g == chips - 1)
                def _():
                    for copy in small:
                        copy.start()

            for v in range(units):

                @pl.when(s == v)
                def _():
                    for copy in w_copies(v):
                        copy.wait()

            parts[s] = jnp.dot(scaled[...], w[u], preferred_element_type=F32)

        reduce_step(s, me, right, 1, qr, kr, er, rsem, resem)
        reduce_step(s, last - me, left, 0, ql, kl, el, lsem, lesem)

        @pl.when((s < count) & (u == 1))
        def _():
            tables(g)

        @pl.when((u == max(0, units - FORWARD)) & (g + 1 < chips))
        def _():
            @pl.when(g + 3 < chips)
            def _():
                for f in range(2):
                    same_copy(g + 3, f).start()

            for part in range(2):
                m, f = member(g + 1, part, chips)
                same_copy(m, f).wait_recv()
                pair_copy(m, f, False).start()

    def drain(j, pos, peer, q_land, k_land, steps, sems, step_sems):
        m, u = lax.div(j, units), lax.rem(j, units)

        @pl.when((pos < last) & (u == 0))
        def _():
            for copy in code_copies(k_land.at[m], steps.at[j], sems, step_sems, j, peer):
                copy.wait_send()

        @pl.when((pos < last) & (u > 0))
        def _():
            jq = m * tiles + u - 1
            for copy in code_copies(q_land.at[jq], steps.at[j], sems, step_sems, j, peer):
                copy.wait_send()

    @pl.loop(0, count)
    def _(j):
        drain(j, me, right, qr, kr, er, rsem, resem)
        drain(j, last - me, left, ql, kl, el, lsem, lesem)

    for m in range(chips):
        for f in range(2):
            pair_copy(jnp.int32(m), f, False).wait_send()
            if m:
                same_copy(jnp.int32(m), f).wait_send()
    for copy in small:
        copy.wait()
    total = sqs[...]
    for d in range(n - 1):
        total = total + lsq[d]
    sqo[...] = total


def front(tokens, gain, w_query, w_key, w_value, seg_rows, rope, n, n_ha):
    rows, width = tokens.shape
    cols = w_query.shape[1]
    chips, tiles = n_ha // 2, cols // TILE
    units = tiles + 1
    count = chips * units
    vmem, any_ = pl.BlockSpec(memory_space=pltpu.VMEM), pl.BlockSpec(memory_space=pl.ANY)
    dma = pltpu.SemaphoreType.DMA
    return pl.pallas_call(
        functools.partial(front_kernel, n, chips, rows, tiles, n_ha // KVH),
        out_shape=(
            jax.ShapeDtypeStruct((chips * tiles, rows, TILE), F32),
            jax.ShapeDtypeStruct((chips, 2 * rows, TILE), F32),
            jax.ShapeDtypeStruct((n_ha, rows), F32),
            jax.ShapeDtypeStruct((n_ha, rows, 2 * HD), F32),
        ),
        in_specs=[any_, vmem, any_, any_, any_, vmem, vmem],
        out_specs=(vmem,) * 4,
        scratch_shapes=[
            pltpu.VMEM((chips, 2 * rows, width), BF16),
            pltpu.VMEM((2 * rows, width), BF16),
            pltpu.VMEM((units, width, TILE), BF16),
            pltpu.VMEM((count, 2 * rows, TILE), F32),
            pltpu.VMEM((chips * tiles, rows, TILE), jnp.int16),
            pltpu.VMEM((chips * tiles, rows, TILE), jnp.int16),
            pltpu.VMEM((chips, 2 * rows, TILE), jnp.int16),
            pltpu.VMEM((chips, 2 * rows, TILE), jnp.int16),
            pltpu.VMEM((count, 8, rows), F32),
            pltpu.VMEM((count, 8, rows), F32),
            pltpu.VMEM((2 * rows, 128), F32),
            pltpu.VMEM((n_ha, rows), F32),
            pltpu.VMEM((n - 1, n_ha, rows), F32),
            dma((units + 1,)),
            dma,
            dma((2, chips, 2)),
            dma((2, chips, 2)),
            dma((2, count)),
            dma((2, count)),
            dma((2, count)),
            dma((2, count)),
            dma((2, n - 1)),
        ],
        compiler_params=pltpu.CompilerParams(
            collective_id=0, has_side_effects=True, vmem_limit_bytes=60 << 20
        ),
    )(tokens, gain, w_query, w_key, w_value, seg_rows, rope)


def back_kernel(
    n, chips, rows, tiles, wides, all_width,
    q_ref, kv_ref, sq_ref, cs_ref, seg_ref, tok_ref, wo_hbm,
    sum_ref, sqo_ref,
    wo, keys, values, mask, qscale, head, acc, got, stage, land, own, sqp, sq2, lsq2,
    wsem, rsem, lsem, psem, xsem, ssem,
):
    me, ha = lax.axis_index("wa"), lax.axis_index("ha")
    core, chip = lax.rem(ha, 2), lax.div(ha, 2)
    last = n - 1
    n_chunk, n_unit = chips * tiles, chips * wides
    lag = tiles + SKEW * last
    hrows = rows // 2
    window = WINDOW + hrows
    end_row = jnp.where(me == last, 1, 0)
    partner = chip * 2 + 1 - core
    mine = pl.ds(pl.multiple_of(core * rows, rows), rows)
    theirs = pl.ds(pl.multiple_of((1 - core) * rows, rows), rows)

    def w_copy(k):
        return pltpu.make_async_copy(wo_hbm.at[:, pl.ds(k * WIDE, WIDE)], wo.at[k], wsem.at[k])

    for k in range(wides):
        w_copy(k).start()
    greet(n, chips, me, chip, core)

    def row_scale(k):
        return column(lax.rsqrt(sq_ref[pl.ds(k, 1), :] / all_width + EPS))

    def rotated(x, cs):
        return x * cs[:, :HD] + pltpu.roll(x, HD // 2, 1) * cs[:, HD:]

    def first_row(g, part, e):
        m, f = member(g, part, chips)
        half = (mirror(chip, m, chips) * 2 + e) * 2 + f
        return half, pl.multiple_of(half * hrows, hrows)

    is_end = (me == 0) | (me == last)

    @pl.when(is_end)
    def _():
        zero = jnp.zeros((WINDOW, HD), BF16)
        keys[pl.ds(0, WINDOW), :] = zero
        values[pl.ds(0, WINDOW), :] = zero

        @pl.loop(0, chips)
        def _(g):
            for e in range(2):
                scale = row_scale(g * 2 + e)
                block = kv_ref.at[g, pl.ds(e * rows, rows)]
                plain = (block[:, :HD] * scale).astype(BF16).astype(F32)
                turned = rotated(plain, cs_ref[g * 2 + e]).astype(BF16)
                value = (block[:, HD:] * scale).astype(BF16)
                for part in range(2):
                    _, row = first_row(g, part, e)
                    at = pl.ds(pl.multiple_of(WINDOW + row, hrows), hrows)
                    cut = slice(part * hrows, (part + 1) * hrows)
                    keys[at, :] = turned[cut]
                    values[at, :] = value[cut]

    def attend(j):
        p, t = lax.div(j, tiles), lax.rem(j, tiles)
        g = chips - 1 - p

        @pl.when(t == 0)
        def _():
            for part in range(2):
                half, _ = first_row(g, part, end_row)
                ones = jnp.where(allowed_mask(seg_ref[half], hrows), 1.0, 0.0)
                mask[part, pl.ds(0, hrows), :] = ones
                mask[part, pl.ds(hrows, hrows), :] = ones
            qscale[...] = jnp.broadcast_to(row_scale(g * 2 + end_row), (rows, HD))

        for part in range(2):
            _, row = first_row(g, part, end_row)
            at = pl.ds(row, window)
            cut = slice(part * hrows, (part + 1) * hrows)
            cs = cs_ref[g * 2 + end_row, cut, :]
            query = jnp.concatenate(
                [
                    rotated(q_ref[g * tiles + t, cut, x * HD : (x + 1) * HD] * qscale[cut, :], cs)
                    for x in range(TILE // HD)
                ],
                axis=0,
            ).astype(BF16)
            allowed = mask[part] > 0.5
            scores = lax.dot_general(
                query, keys[at, :], (((1,), (1,)), ((), ())), preferred_element_type=F32
            ) * HD ** (-0.5)
            scores = jnp.where(allowed, scores, -1e30)
            peak = jnp.max(scores, axis=1, keepdims=True)
            expo = jnp.where(allowed, jnp.exp(scores - peak), 0.0)
            weights = (expo / jnp.sum(expo, axis=1, keepdims=True)).astype(BF16)
            out = jnp.dot(weights, values[at, :], preferred_element_type=F32).astype(BF16)
            to = pl.ds(pl.multiple_of(end_row * rows + part * hrows, hrows), hrows)
            for x in range(TILE // HD):
                head[p, t, to, x * HD : (x + 1) * HD] = out[x * hrows : (x + 1) * hrows]

    def spread_copy(j, e, peer, sems):
        ref = head.at[lax.div(j, tiles), lax.rem(j, tiles), pl.ds(e * rows, rows)]
        return send_to(ref, ref, sems, (j,), wa=peer)

    def spread_step(s, pos, peer, e, sems):
        j = s - SKEW * pos

        @pl.when((j >= 0) & (j < n_chunk))
        def _():
            copy = spread_copy(j, e, peer, sems)

            @pl.when(pos > 0)
            def _():
                copy.wait_recv()

            @pl.when(pos < last)
            def _():
                copy.start()

    def pair_copy(v):
        return send_to(acc.at[lax.rem(v, RING), theirs], got.at[v], psem, (v,), ha=partner)

    def peer_copy(v, part):
        m, _ = member(chips - 1 - lax.div(v, wides), part, chips)
        cut = pl.ds(part * hrows, hrows)
        return send_to(
            stage.at[v, cut], land.at[v, cut], xsem, (v, part),
            ha=mirror(chip, m, chips) * 2 + core,
        )

    def project(v):
        p, k = lax.div(v, wides), lax.rem(v, wides)
        for i in range(wides):

            @pl.when(v == i)
            def _():
                w_copy(i).wait()

        @pl.when(v >= RING)
        def _():
            pair_copy(v - RING).wait_send()

        block = jnp.concatenate([head[p, t] for t in range(tiles)], axis=1)
        for y in range(WIDE // TILE):
            at = slice(y * TILE, (y + 1) * TILE)
            acc[lax.rem(v, RING), :, at] = jnp.dot(
                block, wo[k, :, at], preferred_element_type=F32
            )
        pair_copy(v).start()

    def combine(v):
        p, k = lax.div(v, wides), lax.rem(v, wides)
        pair_copy(v).wait_recv()
        both = acc[lax.rem(v, RING), mine, :] + got[v]

        @pl.when(p < chips - 1)
        def _():
            stage[v] = both.astype(BF16)
            for part in range(2):
                peer_copy(v, part).start()

        @pl.when(p == chips - 1)
        def _():
            own[k] = both

    right, left = jnp.minimum(me + 1, last), jnp.maximum(me - 1, 0)

    @pl.loop(0, n_unit + lag + 1)
    def _(s):
        @pl.when(is_end & (s < n_chunk))
        def _():
            attend(s)

        spread_step(s, me, right, 0, rsem)
        spread_step(s, last - me, left, 1, lsem)

        v = s - lag

        @pl.when((v >= 0) & (v < n_unit))
        def _():
            project(v)

        @pl.when(v >= 1)
        def _():
            combine(v - 1)

    @pl.loop(0, wides)
    def _(k):
        halves = [own[k, pl.ds(f * hrows, hrows), :] for f in range(2)]
        for p in range(chips - 1):
            g, v = chips - 1 - p, p * wides + k
            for part in range(2):
                peer_copy(v, part).wait_recv()
                f = part if g == chips - 1 else (g - 1) % 2
                halves[f] = halves[f] + land[v, pl.ds(part * hrows, hrows), :].astype(F32)
        total = jnp.concatenate(halves, axis=0)
        at = pl.ds(pl.multiple_of(k * WIDE, WIDE), WIDE)
        sum_ref[:, at] = total
        wide = (tok_ref[:, at].astype(F32) + total).astype(BF16).astype(F32)
        square = fold_lanes(wide * wide)

        @pl.when(k == 0)
        def _():
            sqp[...] = square

        @pl.when(k > 0)
        def _():
            sqp[...] = sqp[...] + square

    sq2[...] = lane_sums(sqp[...])
    small = [
        send_to(sq2, lsq2.at[d - 1], ssem, (d - 1,), wa=lax.rem(me + d, n)) for d in range(1, n)
    ]
    for copy in small:
        copy.start()

    @pl.loop(0, n_chunk)
    def _(j):
        @pl.when(me < last)
        def _():
            spread_copy(j, 0, right, rsem).wait_send()

        @pl.when(me > 0)
        def _():
            spread_copy(j, 1, left, lsem).wait_send()

    @pl.loop(0, n_unit - wides)
    def _(v):
        for part in range(2):
            peer_copy(v, part).wait_send()

    for v in range(n_unit - RING, n_unit):
        pair_copy(jnp.int32(v)).wait_send()
    for copy in small:
        copy.wait()
    total = sq2[...]
    for d in range(n - 1):
        total = total + lsq2[d]
    sqo_ref[...] = total


def back(q_sum, kv_sum, sq_sum, cs, seg_rows, tokens, w_out, n, n_ha):
    rows, width = tokens.shape
    cols = w_out.shape[0]
    chips, tiles, wides = n_ha // 2, cols // TILE, width // WIDE
    n_chunk, n_unit = chips * tiles, chips * wides
    vmem, any_ = pl.BlockSpec(memory_space=pltpu.VMEM), pl.BlockSpec(memory_space=pl.ANY)
    dma = pltpu.SemaphoreType.DMA
    return pl.pallas_call(
        functools.partial(back_kernel, n, chips, rows, tiles, wides, width * n),
        out_shape=(
            jax.ShapeDtypeStruct((rows, width), F32),
            jax.ShapeDtypeStruct((8, rows), F32),
        ),
        in_specs=[vmem] * 6 + [any_],
        out_specs=(vmem, vmem),
        scratch_shapes=[
            pltpu.VMEM((wides, cols, WIDE), BF16),
            pltpu.VMEM((WINDOW + n_ha * rows, HD), BF16),
            pltpu.VMEM((WINDOW + n_ha * rows, HD), BF16),
            pltpu.VMEM((2, rows, WINDOW + rows // 2), F32),
            pltpu.VMEM((rows, HD), F32),
            pltpu.VMEM((chips, tiles, 2 * rows, TILE), BF16),
            pltpu.VMEM((RING, 2 * rows, WIDE), F32),
            pltpu.VMEM((n_unit, rows, WIDE), F32),
            pltpu.VMEM((n_unit - wides, rows, WIDE), BF16),
            pltpu.VMEM((n_unit - wides, rows, WIDE), BF16),
            pltpu.VMEM((wides, rows, WIDE), F32),
            pltpu.VMEM((rows, 128), F32),
            pltpu.VMEM((8, rows), F32),
            pltpu.VMEM((n - 1, 8, rows), F32),
            dma((wides,)),
            dma((2, n_chunk)),
            dma((2, n_chunk)),
            dma((2, n_unit)),
            dma((2, n_unit - wides, 2)),
            dma((2, n - 1)),
        ],
        compiler_params=pltpu.CompilerParams(
            collective_id=1, has_side_effects=True, vmem_limit_bytes=60 << 20
        ),
    )(q_sum, kv_sum, sq_sum, cs, seg_rows, tokens, w_out)


def on_device(tokens, gain_attn, w_query, w_key, w_value, w_out, gain_ffn, segment_ids):
    rows, width = tokens.shape
    n_wa = lax.axis_size("wa")
    n_ha = lax.axis_size("ha")
    padded = jnp.pad(segment_ids, (WINDOW, 0), constant_values=-1).astype(F32)
    half = rows // 2
    seg_rows = jnp.stack(
        [padded[None, k * half : (k + 1) * half + WINDOW] for k in range(2 * n_ha)]
    )
    q_sum, kv_sum, sq_sum, cs = front(
        tokens, gain_attn.reshape(1, width), w_query, w_key, w_value, seg_rows, rope_rows(),
        n_wa, n_ha,
    )
    attended, square_two = back(
        q_sum, kv_sum, sq_sum, cs, seg_rows, tokens, w_out, n_wa, n_ha
    )
    residual_out = (tokens.astype(F32) + attended).astype(BF16)
    scale_two = lax.rsqrt(square_two[0] / (width * n_wa) + EPS)
    ffn_input = (
        residual_out.astype(F32) * scale_two[:, None] * gain_ffn.astype(F32)
    ).astype(BF16)
    return (residual_out, ffn_input)


def solution(mesh):
    in_specs = (
        P("ha", "wa"),
        P("wa"),
        P("wa", "ha"),
        P("wa", None),
        P("wa", None),
        P("ha", "wa"),
        P("wa"),
        P(),
    )
    out_specs = (P("ha", "wa"), P("ha", "wa"))
    return jax.shard_map(
        on_device, mesh=mesh, in_specs=in_specs, out_specs=out_specs, check_vma=False
    )
```

```python
import functools

import jax
import jax.numpy as jnp
from jax import lax
from jax.experimental import pallas as pl
from jax.experimental.pallas import tpu as pltpu
from jax.sharding import PartitionSpec as P

KVH = 8
HD = 128
WINDOW = 256
EPS = 1e-05
TILE = 256
WIDE = 512
SKEW = 3
SPREAD_SKEW = 3
LEVELS = 32766.0
FORWARD = 2
RING = 4
DEEP = 8
F32 = jnp.float32
BF16 = jnp.bfloat16


def rope_rows():
    half = HD // 2
    inverse = 500000.0 ** (-(jnp.arange(half, dtype=F32) * 2.0 / HD))
    angle = jnp.arange(WINDOW, dtype=F32)[:, None] * inverse[None, :]
    cosine, sine = jnp.cos(angle), jnp.sin(angle)
    return jnp.concatenate([cosine, cosine, -sine, sine], axis=1)


def mirror(a, m, size):
    total, bit = 0, 1
    while bit < size:
        total = total + lax.rem(lax.div(a, bit) + lax.div(m, bit), 2) * bit
        bit *= 2
    return total


def member(g, sub, chips):
    edge = (g == 0) | (g == chips - 1)
    low = lax.div(g - 1, 2) * 2 + 1
    return jnp.where(edge, g, low + sub), jnp.where(edge, sub, lax.rem(g - 1, 2))


def place(m, f, chips):
    edge = (m == 0) | (m == chips - 1)
    low = lax.div(m - 1, 2) * 2 + 1
    return jnp.where(edge, m, low + f), jnp.where(edge, f, lax.rem(m - 1, 2))


def send_to(src, dst, sems, at, **peer):
    return pltpu.make_async_remote_copy(
        src_ref=src,
        dst_ref=dst,
        send_sem=sems.at[(0,) + at],
        recv_sem=sems.at[(1,) + at],
        device_id=peer,
        device_id_type=pl.DeviceIdType.MESH,
    )


def greet(n, chips, me, chip, core):
    barrier = pltpu.get_barrier_semaphore()

    def signal(**peer):
        pl.semaphore_signal(
            barrier, inc=1, device_id=peer, device_id_type=pl.DeviceIdType.MESH
        )

    for d in range(1, n):
        signal(wa=lax.rem(me + d, n))
    for m in range(1, chips):
        signal(ha=mirror(chip, jnp.int32(m), chips) * 2 + core)
    signal(ha=chip * 2 + 1 - core)
    pl.semaphore_wait(barrier, n + chips - 1)


def column(row):
    r = row.shape[1]
    a = lax.broadcasted_iota(jnp.int32, (r, r), 0)
    b = lax.broadcasted_iota(jnp.int32, (r, r), 1)
    return jnp.sum(jnp.where(a == b, jnp.broadcast_to(row, (r, r)), 0.0), axis=1, keepdims=True)


def as_row(col):
    r = col.shape[0]
    a = lax.broadcasted_iota(jnp.int32, (r, r), 0)
    b = lax.broadcasted_iota(jnp.int32, (r, r), 1)
    return jnp.sum(jnp.where(a == b, jnp.broadcast_to(col, (r, r)), 0.0), axis=0, keepdims=True)


def encode(x, code, steps, rows):
    for i in range(x.shape[0] // rows):
        for y in range(TILE // HD):
            part = x[i * rows : (i + 1) * rows, y * HD : (y + 1) * HD]
            top = jnp.maximum(jnp.max(jnp.abs(part), axis=1, keepdims=True), 1e-30)
            whole = jnp.round(part * (LEVELS / top)).astype(jnp.int32)
            code[i * rows : (i + 1) * rows, y * HD : (y + 1) * HD] = whole.astype(jnp.int16)
            k = i * 2 + y
            steps[k : k + 1, :] = as_row(top * (1.0 / LEVELS))


def decode(code, steps, rows):
    blocks = []
    for i in range(code.shape[0] // rows):
        line = []
        for y in range(TILE // HD):
            part = code[i * rows : (i + 1) * rows, y * HD : (y + 1) * HD]
            k = i * 2 + y
            line.append(part.astype(jnp.int32).astype(F32) * column(steps[k : k + 1, :]))
        blocks.append(jnp.concatenate(line, axis=1))
    return jnp.concatenate(blocks, axis=0)


def lane_sums(block):
    ones = jnp.ones((8, block.shape[1]), F32)
    return lax.dot_general(
        ones, block, (((1,), (1,)), ((), ())), precision=lax.Precision.HIGHEST,
        preferred_element_type=F32,
    )


def fold_lanes(x):
    total = x[:, :128]
    for g in range(1, x.shape[1] // 128):
        total = total + x[:, g * 128 : (g + 1) * 128]
    return total


def allowed_mask(seg_row, rows):
    keys = seg_row.shape[1]
    q_seg = column(seg_row[:, keys - rows :])
    q_at = lax.broadcasted_iota(jnp.int32, (rows, keys), 0) + (keys - rows)
    k_at = lax.broadcasted_iota(jnp.int32, (rows, keys), 1)
    return (q_seg == seg_row) & (k_at <= q_at)


def plan(n, chips, tiles, wides):
    units = tiles + 1
    start = 0
    for p in range(chips):
        g = (p + 1) % chips
        start = max(start, (g + 1) * units + SKEW * (n - 1) - p * tiles)
    start = max(start, (chips - 1) * units + SKEW * (n - 1) + 1)
    lag = max(0, tiles - wides) * chips + tiles + SPREAD_SKEW * (n - 1)
    return start, lag


def layer_kernel(
    n, chips, rows, tiles, wides, per_head, all_width,
    tok_hbm, gain_ref, wq_hbm, wk_hbm, wv_hbm, seg_ref, rope_ref, tok_ref, wo_hbm,
    sum_ref, scale_ref,
    tok, scaled, w, parts, qr, ql, kr, kl, er, el, cs, sqp, sqs, lsq,
    keys, values, mask, qscale, head, acc, got, own, sq2, lsq2,
    wsem, tsem, same_sem, pair_sem, rsem, lsem, resem, lesem, ssem,
    osem, srsem, slsem, psem, xsem, s2sem, free_sem, credit_sem,
):
    me, ha = lax.axis_index("wa"), lax.axis_index("ha")
    core, chip = lax.rem(ha, 2), lax.div(ha, 2)
    last = n - 1
    units = tiles + 1
    count = chips * units
    n_chunk, n_unit = chips * tiles, chips * wides
    start, lag = plan(n, chips, tiles, wides)
    hrows = rows // 2
    window = WINDOW + hrows
    cols = tiles * TILE
    fold = w.shape[1] // cols
    own_at = pl.multiple_of(core * rows, rows)
    kv_at = pl.multiple_of(lax.div(ha, per_head) * HD, HD)
    partner = chip * 2 + 1 - core
    mine = pl.ds(own_at, rows)
    theirs = pl.ds(pl.multiple_of((1 - core) * rows, rows), rows)
    right, left = jnp.minimum(me + 1, last), jnp.maximum(me - 1, 0)
    end_row = jnp.where(me == last, 1, 0)
    is_end = (me == 0) | (me == last)

    def w_copies(u):
        if u == 0:
            return [
                pltpu.make_async_copy(
                    wk_hbm.at[:, pl.ds(kv_at, HD)], w.at[0, :, pl.ds(0, HD)], wsem.at[0]
                ),
                pltpu.make_async_copy(
                    wv_hbm.at[:, pl.ds(kv_at, HD)], w.at[0, :, pl.ds(HD, HD)], wsem.at[1]
                ),
            ]
        return [
            pltpu.make_async_copy(
                wq_hbm.at[:, pl.ds((u - 1) * TILE, TILE)], w.at[u], wsem.at[u + 1]
            )
        ]

    def wo_copy(c):
        return pltpu.make_async_copy(
            wo_hbm.at[:, pl.ds(c * TILE, TILE)],
            w.at[c // fold, pl.ds((c % fold) * cols, cols)],
            osem.at[c],
        )

    n_wo = wides * (WIDE // TILE)

    own_copy = pltpu.make_async_copy(tok_hbm, tok.at[0, mine], tsem)
    own_copy.start()
    for u in range(units):
        for copy in w_copies(u):
            copy.start()
    greet(n, chips, me, chip, core)

    def half_rows(f):
        return pl.ds(pl.multiple_of(f * hrows, hrows), hrows)

    def spot(m, f):
        g, part = place(m, f, chips)
        return tok.at[g, pl.ds(pl.multiple_of(own_at + part * hrows, hrows), hrows)]

    def same_copy(m, f):
        return send_to(
            tok_hbm.at[half_rows(f)], spot(m, f), same_sem, (m, f),
            ha=mirror(chip, m, chips) * 2 + core,
        )

    def pair_copy(m, f, first):
        src = tok_hbm.at[half_rows(f)] if first else spot(m, f)
        return send_to(src, spot(m, f), pair_sem, (m, f), ha=partner)

    for f in range(2):
        pair_copy(jnp.int32(0), f, True).start()
    for f in range(2):
        for m in range(1, min(3, chips)):
            same_copy(jnp.int32(m), f).start()

    def peers(src, dst, sems):
        return [
            send_to(src, dst.at[d - 1], sems, (d - 1,), wa=lax.rem(me + d, n))
            for d in range(1, n)
        ]

    small, small_two = peers(sqs, lsq, ssem), peers(sq2, lsq2, s2sem)

    def prepare(g):
        @pl.loop(0, 2 * rows // 16)
        def _(i):
            at = pl.ds(pl.multiple_of(i * 16, 16), 16)
            x = tok[g, at, :].astype(F32)
            scaled[at, :] = (x * gain_ref[...].astype(F32)).astype(BF16)
            sqp[at, :] = fold_lanes(x * x)

        for e in range(2):
            sqs[pl.ds(g * 2 + e, 1), :] = lane_sums(sqp[pl.ds(e * rows, rows), :])[:1]

    def tables(g):
        for e in range(2):
            for part in range(2):
                m, f = member(g, part, chips)
                allowed = allowed_mask(seg_ref[(mirror(chip, m, chips) * 2 + e) * 2 + f], hrows)
                at = jnp.sum(jnp.where(allowed, 1.0, 0.0), axis=1, keepdims=True) - 1.0
                lanes = lax.broadcasted_iota(jnp.int32, (hrows, WINDOW), 1)
                pick = jnp.where(lanes == at.astype(jnp.int32), 1.0, 0.0)
                cs[g * 2 + e, part * hrows : (part + 1) * hrows, :] = jnp.dot(
                    pick, rope_ref[...], precision=lax.Precision.HIGHEST,
                    preferred_element_type=F32,
                )

    def code_copies(land, steps, sems, step_sems, j, peer):
        return (
            send_to(land, land, sems, (j,), wa=peer),
            send_to(steps, steps, step_sems, (j,), wa=peer),
        )

    def handle(pos, peer, part, land, steps, sems, step_sems, j):
        copies = code_copies(land, steps, sems, step_sems, j, peer)

        @pl.when(pos == 0)
        def _():
            encode(part[...], land, steps, rows)

        @pl.when(pos > 0)
        def _():
            for copy in copies:
                copy.wait_recv()

        @pl.when((pos > 0) & (pos < last))
        def _():
            encode(decode(land, steps, rows) + part[...], land, steps, rows)

        @pl.when(pos < last)
        def _():
            for copy in copies:
                copy.start()

        @pl.when(pos == last)
        def _():
            part[...] = decode(land, steps, rows) + part[...]

    def reduce_step(s, pos, peer, e, q_land, k_land, steps, sems, step_sems):
        j = s - SKEW * pos

        @pl.when((j >= 0) & (j < count))
        def _():
            g, u = lax.div(j, units), lax.rem(j, units)

            @pl.when(u == 0)
            def _():
                handle(
                    pos, peer, parts.at[j], k_land.at[g], steps.at[j], sems, step_sems, j
                )

            @pl.when(u > 0)
            def _():
                jq = g * tiles + u - 1
                part = parts.at[j, pl.ds(e * rows, rows)]
                handle(pos, peer, part, q_land.at[jq], steps.at[j], sems, step_sems, j)

    def front_step(s):
        g, u = lax.div(s, units), lax.rem(s, units)

        @pl.when(s < count)
        def _():
            @pl.when(u == 0)
            def _():
                @pl.when(g == 0)
                def _():
                    own_copy.wait()

                for part in range(2):
                    pair_copy(*member(g, part, chips), False).wait_recv()
                prepare(g)

                @pl.when(g == chips - 1)
                def _():
                    for copy in small:
                        copy.start()

            for v in range(units):

                @pl.when(s == v)
                def _():
                    for copy in w_copies(v):
                        copy.wait()

            parts[s] = jnp.dot(scaled[...], w[u], preferred_element_type=F32)

        @pl.when(s == count)
        def _():
            for c in range(n_wo):
                wo_copy(c).start()

        reduce_step(s, me, right, 1, qr, kr, er, rsem, resem)
        reduce_step(s, last - me, left, 0, ql, kl, el, lsem, lesem)

        @pl.when((s < count) & (u == 1))
        def _():
            tables(g)

        @pl.when((u == max(0, units - FORWARD)) & (g + 1 < chips))
        def _():
            @pl.when(g + 3 < chips)
            def _():
                for f in range(2):
                    same_copy(g + 3, f).start()

            for part in range(2):
                m, f = member(g + 1, part, chips)
                same_copy(m, f).wait_recv()
                pair_copy(m, f, False).start()

    def drain(j, pos, peer, q_land, k_land, steps, sems, step_sems):
        g, u = lax.div(j, units), lax.rem(j, units)

        @pl.when((pos < last) & (u == 0))
        def _():
            for copy in code_copies(k_land.at[g], steps.at[j], sems, step_sems, j, peer):
                copy.wait_send()

        @pl.when((pos < last) & (u > 0))
        def _():
            jq = g * tiles + u - 1
            for copy in code_copies(q_land.at[jq], steps.at[j], sems, step_sems, j, peer):
                copy.wait_send()

    def group(p):
        return lax.rem(p + 1, chips)

    def row_scale(k):
        return column(lax.rsqrt(sqs[pl.ds(k, 1), :] / all_width + EPS))

    def rotated(x, turn):
        return x * turn[:, :HD] + pltpu.roll(x, HD // 2, 1) * turn[:, HD:]

    def first_row(g, part, e):
        m, f = member(g, part, chips)
        half = (mirror(chip, m, chips) * 2 + e) * 2 + f
        return half, pl.multiple_of(half * hrows, hrows)

    def settle():
        for m in range(chips):
            for f in range(2):
                pair_copy(jnp.int32(m), f, False).wait_send()
                if m:
                    same_copy(jnp.int32(m), f).wait_send()
        for m in range(1, chips):
            pl.semaphore_signal(
                free_sem, inc=1,
                device_id={"ha": mirror(chip, jnp.int32(m), chips) * 2 + core},
                device_id_type=pl.DeviceIdType.MESH,
            )
        for copy in small:
            copy.wait()
        total = sqs[...]
        for d in range(n - 1):
            total = total + lsq[d]
        sqs[...] = total

        @pl.when(is_end)
        def _():
            zero = jnp.zeros((WINDOW, HD), BF16)
            keys[pl.ds(0, WINDOW), :] = zero
            values[pl.ds(0, WINDOW), :] = zero

            @pl.loop(0, chips)
            def _(g):
                for e in range(2):
                    scale = row_scale(g * 2 + e)
                    block = parts.at[g * units, pl.ds(e * rows, rows)]
                    plain = (block[:, :HD] * scale).astype(BF16).astype(F32)
                    turned = rotated(plain, cs[g * 2 + e]).astype(BF16)
                    value = (block[:, HD:] * scale).astype(BF16)
                    for part in range(2):
                        _, row = first_row(g, part, e)
                        at = pl.ds(pl.multiple_of(WINDOW + row, hrows), hrows)
                        cut = slice(part * hrows, (part + 1) * hrows)
                        keys[at, :] = turned[cut]
                        values[at, :] = value[cut]

    def attend(j):
        p, t = lax.div(j, tiles), lax.rem(j, tiles)
        g = group(p)

        @pl.when(t == 0)
        def _():
            for part in range(2):
                half, _ = first_row(g, part, end_row)
                ones = jnp.where(allowed_mask(seg_ref[half], hrows), 1.0, 0.0)
                mask[part, pl.ds(0, hrows), :] = ones
                mask[part, pl.ds(hrows, hrows), :] = ones
            qscale[...] = jnp.broadcast_to(row_scale(g * 2 + end_row), (rows, HD))

        for part in range(2):
            _, row = first_row(g, part, end_row)
            at = pl.ds(row, window)
            cut = slice(part * hrows, (part + 1) * hrows)
            to = pl.ds(pl.multiple_of(end_row * rows + part * hrows, hrows), hrows)
            turn = cs[g * 2 + end_row, cut, :]
            query = jnp.concatenate(
                [
                    rotated(
                        parts[g * units + 1 + t, to, x * HD : (x + 1) * HD] * qscale[cut, :], turn
                    )
                    for x in range(TILE // HD)
                ],
                axis=0,
            ).astype(BF16)
            allowed = mask[part] > 0.5
            scores = lax.dot_general(
                query, keys[at, :], (((1,), (1,)), ((), ())), preferred_element_type=F32
            ) * HD ** (-0.5)
            scores = jnp.where(allowed, scores, -1e30)
            peak = jnp.max(scores, axis=1, keepdims=True)
            expo = jnp.where(allowed, jnp.exp(scores - peak), 0.0)
            weights = (expo / jnp.sum(expo, axis=1, keepdims=True)).astype(BF16)
            out = jnp.dot(weights, values[at, :], preferred_element_type=F32).astype(BF16)
            for x in range(TILE // HD):
                head[p, t, to, x * HD : (x + 1) * HD] = out[x * hrows : (x + 1) * hrows]

    def spread_copy(j, e, peer, sems):
        ref = head.at[lax.div(j, tiles), lax.rem(j, tiles), pl.ds(e * rows, rows)]
        return send_to(ref, ref, sems, (j,), wa=peer)

    def spread_step(s, pos, peer, e, sems):
        j = s - SPREAD_SKEW * pos

        @pl.when((j >= 0) & (j < n_chunk))
        def _():
            copy = spread_copy(j, e, peer, sems)

            @pl.when(pos > 0)
            def _():
                copy.wait_recv()

            @pl.when(pos < last)
            def _():
                copy.start()

    def swap_copy(v):
        return send_to(
            acc.at[lax.rem(v, RING), theirs], got.at[lax.rem(v, DEEP)], psem, (v,), ha=partner
        )

    def stage(v, part):
        p, k = lax.div(v, wides), lax.rem(v, wides)
        at = pl.ds(pl.multiple_of(k * WIDE, WIDE), WIDE)
        return tok.at[p, pl.ds(rows + part * hrows, hrows), at]

    def land(v, part):
        p, k = lax.div(v, wides), lax.rem(v, wides)
        at = pl.ds(pl.multiple_of(k * WIDE, WIDE), WIDE)
        return tok.at[p, pl.ds(part * hrows, hrows), at]

    def peer_copy(v, part):
        m, _ = member(group(lax.div(v, wides)), part, chips)
        return send_to(
            stage(v, part), land(v, part), xsem, (v, part), ha=mirror(chip, m, chips) * 2 + core
        )

    def project(v):
        p, k = lax.div(v, wides), lax.rem(v, wides)

        @pl.when(v == 0)
        def _():
            for c in range(n_wo):
                wo_copy(c).wait()

        @pl.when(v >= RING)
        def _():
            swap_copy(v - RING).wait_send()

        block = jnp.concatenate([head[p, t] for t in range(tiles)], axis=1)
        for y in range(WIDE // TILE):
            c = k * (WIDE // TILE) + y
            deep = pl.ds(pl.multiple_of(lax.rem(c, fold) * cols, cols), cols)
            acc[lax.rem(v, RING), :, y * TILE : (y + 1) * TILE] = jnp.dot(
                block, w[lax.div(c, fold), deep, :], preferred_element_type=F32
            )

        @pl.when(v >= DEEP)
        def _():
            pl.semaphore_wait(credit_sem, 1)

        swap_copy(v).start()

    def combine(v):
        p, k = lax.div(v, wides), lax.rem(v, wides)
        swap_copy(v).wait_recv()
        both = acc[lax.rem(v, RING), mine, :] + got[lax.rem(v, DEEP)]

        @pl.when(v + DEEP < n_unit)
        def _():
            pl.semaphore_signal(
                credit_sem, inc=1, device_id={"ha": partner},
                device_id_type=pl.DeviceIdType.MESH,
            )

        @pl.when(v == 0)
        def _():
            pl.semaphore_wait(free_sem, chips - 1)

        @pl.when(p < chips - 1)
        def _():
            for part in range(2):
                stage(v, part)[...] = both[part * hrows : (part + 1) * hrows].astype(BF16)
                peer_copy(v, part).start()

        @pl.when(p == chips - 1)
        def _():
            own[k] = both

    @pl.loop(0, start + lag + n_unit + 1)
    def _(s):
        @pl.when(s < count + SKEW * last)
        def _():
            front_step(s)

        @pl.when(s == start)
        def _():
            settle()

        r = s - start

        @pl.when(r >= 0)
        def _():
            @pl.when(is_end & (r < n_chunk))
            def _():
                attend(r)

            spread_step(r, me, right, 0, srsem)
            spread_step(r, last - me, left, 1, slsem)

        v = r - lag

        @pl.when((v >= 0) & (v < n_unit))
        def _():
            project(v)

        @pl.when(v >= 1)
        def _():
            combine(v - 1)

    @pl.loop(0, wides)
    def _(k):
        halves = [own[k, pl.ds(f * hrows, hrows), :] for f in range(2)]
        for p in range(chips - 1):
            g, v = p + 1, p * wides + k
            for part in range(2):
                peer_copy(v, part).wait_recv()
                f = part if g == chips - 1 else (g - 1) % 2
                halves[f] = halves[f] + land(v, part)[...].astype(F32)
        total = jnp.concatenate(halves, axis=0)
        at = pl.ds(pl.multiple_of(k * WIDE, WIDE), WIDE)
        sum_ref[:, at] = total
        wide = (tok_ref[:, at].astype(F32) + total).astype(BF16).astype(F32)
        square = fold_lanes(wide * wide)

        @pl.when(k == 0)
        def _():
            sqp[pl.ds(0, rows), :] = square

        @pl.when(k > 0)
        def _():
            sqp[pl.ds(0, rows), :] = sqp[pl.ds(0, rows), :] + square

    sq2[...] = lane_sums(sqp[pl.ds(0, rows), :])
    for copy in small_two:
        copy.start()

    @pl.loop(0, count)
    def _(j):
        drain(j, me, right, qr, kr, er, rsem, resem)
        drain(j, last - me, left, ql, kl, el, lsem, lesem)

    @pl.loop(0, n_chunk)
    def _(j):
        @pl.when(me < last)
        def _():
            spread_copy(j, 0, right, srsem).wait_send()

        @pl.when(me > 0)
        def _():
            spread_copy(j, 1, left, slsem).wait_send()

    @pl.loop(0, n_unit - wides)
    def _(v):
        for part in range(2):
            peer_copy(v, part).wait_send()

    for v in range(n_unit - RING, n_unit):
        swap_copy(jnp.int32(v)).wait_send()
    for copy in small_two:
        copy.wait()
    total = sq2[...]
    for d in range(n - 1):
        total = total + lsq2[d]
    scale_ref[...] = jnp.broadcast_to(
        column(lax.rsqrt(total[:1] / all_width + EPS)), scale_ref.shape
    )


def layer(tokens, gain, w_query, w_key, w_value, seg_rows, rope, w_out, n, n_ha):
    rows, width = tokens.shape
    cols = w_query.shape[1]
    chips, tiles, wides = n_ha // 2, cols // TILE, width // WIDE
    units = tiles + 1
    count = chips * units
    n_chunk, n_unit = chips * tiles, chips * wides
    vmem, any_ = pl.BlockSpec(memory_space=pltpu.VMEM), pl.BlockSpec(memory_space=pl.ANY)
    dma, reg = pltpu.SemaphoreType.DMA, pltpu.SemaphoreType.REGULAR
    i16 = jnp.int16
    return pl.pallas_call(
        functools.partial(
            layer_kernel, n, chips, rows, tiles, wides, n_ha // KVH, width * n
        ),
        out_shape=(
            jax.ShapeDtypeStruct((rows, width), F32),
            jax.ShapeDtypeStruct((rows, 128), F32),
        ),
        in_specs=[any_, vmem, any_, any_, any_, vmem, vmem, vmem, any_],
        out_specs=(vmem, vmem),
        scratch_shapes=[
            pltpu.VMEM((chips, 2 * rows, width), BF16),
            pltpu.VMEM((2 * rows, width), BF16),
            pltpu.VMEM((units, width, TILE), BF16),
            pltpu.VMEM((count, 2 * rows, TILE), F32),
            pltpu.VMEM((chips * tiles, rows, TILE), i16),
            pltpu.VMEM((chips * tiles, rows, TILE), i16),
            pltpu.VMEM((chips, 2 * rows, TILE), i16),
            pltpu.VMEM((chips, 2 * rows, TILE), i16),
            pltpu.VMEM((count, 4, rows), F32),
            pltpu.VMEM((count, 4, rows), F32),
            pltpu.VMEM((n_ha, rows, 2 * HD), F32),
            pltpu.VMEM((2 * rows, 128), F32),
            pltpu.VMEM((n_ha, rows), F32),
            pltpu.VMEM((n - 1, n_ha, rows), F32),
            pltpu.VMEM((WINDOW + n_ha * rows, HD), BF16),
            pltpu.VMEM((WINDOW + n_ha * rows, HD), BF16),
            pltpu.VMEM((2, rows, WINDOW + rows // 2), F32),
            pltpu.VMEM((rows, HD), F32),
            pltpu.VMEM((chips, tiles, 2 * rows, TILE), BF16),
            pltpu.VMEM((RING, 2 * rows, WIDE), F32),
            pltpu.VMEM((DEEP, rows, WIDE), F32),
            pltpu.VMEM((wides, rows, WIDE), F32),
            pltpu.VMEM((8, rows), F32),
            pltpu.VMEM((n - 1, 8, rows), F32),
            dma((units + 1,)),
            dma,
            dma((2, chips, 2)),
            dma((2, chips, 2)),
            dma((2, count)),
            dma((2, count)),
            dma((2, count)),
            dma((2, count)),
            dma((2, n - 1)),
            dma((wides * (WIDE // TILE),)),
            dma((2, n_chunk)),
            dma((2, n_chunk)),
            dma((2, n_unit)),
            dma((2, n_unit - wides, 2)),
            dma((2, n - 1)),
            reg,
            reg,
        ],
        compiler_params=pltpu.CompilerParams(
            collective_id=0, has_side_effects=True, vmem_limit_bytes=63 << 20
        ),
    )(tokens, gain, w_query, w_key, w_value, seg_rows, rope, tokens, w_out)


def on_device(tokens, gain_attn, w_query, w_key, w_value, w_out, gain_ffn, segment_ids):
    rows, width = tokens.shape
    n_wa = lax.axis_size("wa")
    n_ha = lax.axis_size("ha")
    padded = jnp.pad(segment_ids, (WINDOW, 0), constant_values=-1).astype(F32)
    half = rows // 2
    seg_rows = jnp.stack(
        [padded[None, k * half : (k + 1) * half + WINDOW] for k in range(2 * n_ha)]
    )
    attended, scale_two = layer(
        tokens, gain_attn.reshape(1, width), w_query, w_key, w_value, seg_rows, rope_rows(),
        w_out, n_wa, n_ha,
    )
    residual_out = (tokens.astype(F32) + attended).astype(BF16)
    ffn_input = (
        residual_out.astype(F32) * scale_two[:, :1] * gain_ffn.astype(F32)
    ).astype(BF16)
    return (residual_out, ffn_input)


def solution(mesh):
    in_specs = (
        P("ha", "wa"),
        P("wa"),
        P("wa", "ha"),
        P("wa", None),
        P("wa", None),
        P("ha", "wa"),
        P("wa"),
        P(),
    )
    out_specs = (P("ha", "wa"), P("ha", "wa"))
    return jax.shard_map(
        on_device, mesh=mesh, in_specs=in_specs, out_specs=out_specs, check_vma=False
    )
```

```python
import functools

import jax
import jax.numpy as jnp
from jax import lax
from jax.experimental import pallas as pl
from jax.experimental.pallas import tpu as pltpu
from jax.sharding import PartitionSpec as P

KVH = 8
HD = 128
WINDOW = 256
EPS = 1e-05
TILE = 256
WIDE = 512
SKEW = 4
SPREAD_SKEW = 3
LEVELS = 32766.0
FORWARD = 3
RING = 4
DEEP = 8
F32 = jnp.float32
BF16 = jnp.bfloat16


def rope_rows():
    half = HD // 2
    inverse = 500000.0 ** (-(jnp.arange(half, dtype=F32) * 2.0 / HD))
    angle = jnp.arange(WINDOW, dtype=F32)[:, None] * inverse[None, :]
    cosine, sine = jnp.cos(angle), jnp.sin(angle)
    return jnp.concatenate([cosine, cosine, -sine, sine], axis=1)


def mirror(a, m, size):
    total, bit = 0, 1
    while bit < size:
        total = total + lax.rem(lax.div(a, bit) + lax.div(m, bit), 2) * bit
        bit *= 2
    return total


def member(g, sub, chips):
    edge = (g == 0) | (g == chips - 1)
    low = lax.div(g - 1, 2) * 2 + 1
    return jnp.where(edge, g, low + sub), jnp.where(edge, sub, lax.rem(g - 1, 2))


def place(m, f, chips):
    edge = (m == 0) | (m == chips - 1)
    low = lax.div(m - 1, 2) * 2 + 1
    return jnp.where(edge, m, low + f), jnp.where(edge, f, lax.rem(m - 1, 2))


def send_to(src, dst, sems, at, **peer):
    return pltpu.make_async_remote_copy(
        src_ref=src,
        dst_ref=dst,
        send_sem=sems.at[(0,) + at],
        recv_sem=sems.at[(1,) + at],
        device_id=peer,
        device_id_type=pl.DeviceIdType.MESH,
    )


def greet(n, chips, me, chip, core):
    barrier = pltpu.get_barrier_semaphore()

    def signal(**peer):
        pl.semaphore_signal(
            barrier, inc=1, device_id=peer, device_id_type=pl.DeviceIdType.MESH
        )

    for d in range(1, n):
        signal(wa=lax.rem(me + d, n))
    for m in range(1, chips):
        signal(ha=mirror(chip, jnp.int32(m), chips) * 2 + core)
    signal(ha=chip * 2 + 1 - core)
    pl.semaphore_wait(barrier, n + chips - 1)


def column(row):
    r = row.shape[1]
    a = lax.broadcasted_iota(jnp.int32, (r, r), 0)
    b = lax.broadcasted_iota(jnp.int32, (r, r), 1)
    return jnp.sum(jnp.where(a == b, jnp.broadcast_to(row, (r, r)), 0.0), axis=1, keepdims=True)


def as_row(col):
    r = col.shape[0]
    a = lax.broadcasted_iota(jnp.int32, (r, r), 0)
    b = lax.broadcasted_iota(jnp.int32, (r, r), 1)
    return jnp.sum(jnp.where(a == b, jnp.broadcast_to(col, (r, r)), 0.0), axis=0, keepdims=True)


def encode(x, code, steps, rows):
    for i in range(x.shape[0] // rows):
        for y in range(TILE // HD):
            part = x[i * rows : (i + 1) * rows, y * HD : (y + 1) * HD]
            top = jnp.maximum(jnp.max(jnp.abs(part), axis=1, keepdims=True), 1e-30)
            whole = jnp.round(part * (LEVELS / top)).astype(jnp.int32)
            code[i * rows : (i + 1) * rows, y * HD : (y + 1) * HD] = whole.astype(jnp.int16)
            k = i * 2 + y
            steps[k : k + 1, :] = as_row(top * (1.0 / LEVELS))


def decode(code, steps, rows):
    blocks = []
    for i in range(code.shape[0] // rows):
        line = []
        for y in range(TILE // HD):
            part = code[i * rows : (i + 1) * rows, y * HD : (y + 1) * HD]
            k = i * 2 + y
            line.append(part.astype(jnp.int32).astype(F32) * column(steps[k : k + 1, :]))
        blocks.append(jnp.concatenate(line, axis=1))
    return jnp.concatenate(blocks, axis=0)


def lane_sums(block):
    ones = jnp.ones((8, block.shape[1]), F32)
    return lax.dot_general(
        ones, block, (((1,), (1,)), ((), ())), precision=lax.Precision.HIGHEST,
        preferred_element_type=F32,
    )


def fold_lanes(x):
    total = x[:, :128]
    for g in range(1, x.shape[1] // 128):
        total = total + x[:, g * 128 : (g + 1) * 128]
    return total


def allowed_mask(seg_row, rows):
    keys = seg_row.shape[1]
    q_seg = column(seg_row[:, keys - rows :])
    q_at = lax.broadcasted_iota(jnp.int32, (rows, keys), 0) + (keys - rows)
    k_at = lax.broadcasted_iota(jnp.int32, (rows, keys), 1)
    return (q_seg == seg_row) & (k_at <= q_at)


def plan(n, chips, tiles, wides):
    units = tiles + 1
    start = (chips - 1) * units + SKEW * (n - 1)
    lag = max(0, tiles - wides) * chips + tiles + SPREAD_SKEW * (n - 1)
    return start, lag


def layer_kernel(
    n, chips, rows, tiles, wides, per_head, all_width,
    tok_hbm, gain_ref, wq_hbm, wk_hbm, wv_hbm, seg_ref, rope_ref, tok_ref, wo_hbm,
    sum_ref, scale_ref,
    tok, scaled, w, parts, qr, ql, kr, kl, er, el, cs, sqp, sqs, lsq,
    keys, values, mask, qscale, head, acc, got, own, sq2, lsq2,
    wsem, tsem, same_sem, pair_sem, rsem, lsem, resem, lesem, ssem,
    osem, srsem, slsem, psem, xsem, s2sem, free_sem, credit_sem,
):
    me, ha = lax.axis_index("wa"), lax.axis_index("ha")
    core, chip = lax.rem(ha, 2), lax.div(ha, 2)
    last = n - 1
    units = tiles + 1
    count = chips * units
    n_chunk, n_unit = chips * tiles, chips * wides
    start, lag = plan(n, chips, tiles, wides)
    hrows = rows // 2
    window = WINDOW + hrows
    cols = tiles * TILE
    fold = w.shape[1] // cols
    own_at = pl.multiple_of(core * rows, rows)
    kv_at = pl.multiple_of(lax.div(ha, per_head) * HD, HD)
    partner = chip * 2 + 1 - core
    mine = pl.ds(own_at, rows)
    theirs = pl.ds(pl.multiple_of((1 - core) * rows, rows), rows)
    right, left = jnp.minimum(me + 1, last), jnp.maximum(me - 1, 0)
    end_row = jnp.where(me == last, 1, 0)
    is_end = (me == 0) | (me == last)
    relay = chips == 4
    order = ([1, chips - 1] + list(range(2, chips - 1)))[: chips - 1] + [0]

    def w_copies(u):
        if u == 0:
            return [
                pltpu.make_async_copy(
                    wk_hbm.at[:, pl.ds(kv_at, HD)], w.at[0, :, pl.ds(0, HD)], wsem.at[0]
                ),
                pltpu.make_async_copy(
                    wv_hbm.at[:, pl.ds(kv_at, HD)], w.at[0, :, pl.ds(HD, HD)], wsem.at[1]
                ),
            ]
        return [
            pltpu.make_async_copy(
                wq_hbm.at[:, pl.ds((u - 1) * TILE, TILE)], w.at[u], wsem.at[u + 1]
            )
        ]

    def wo_copy(c):
        return pltpu.make_async_copy(
            wo_hbm.at[:, pl.ds(c * TILE, TILE)],
            w.at[c // fold, pl.ds((c % fold) * cols, cols)],
            osem.at[c],
        )

    n_wo = wides * (WIDE // TILE)

    own_copy = pltpu.make_async_copy(tok_hbm, tok.at[0, mine], tsem)
    own_copy.start()
    for u in range(units):
        for copy in w_copies(u):
            copy.start()
    greet(n, chips, me, chip, core)

    def half_rows(f):
        return pl.ds(pl.multiple_of(f * hrows, hrows), hrows)

    def spot(m, f):
        g, part = place(m, f, chips)
        return tok.at[g, pl.ds(pl.multiple_of(own_at + part * hrows, hrows), hrows)]

    def same_copy(m, f):
        return send_to(
            tok_hbm.at[half_rows(f)], spot(m, f), same_sem, (m, f),
            ha=mirror(chip, m, chips) * 2 + core,
        )

    def pair_copy(m, f, first):
        src = tok_hbm.at[half_rows(f)] if first else spot(m, f)
        return send_to(src, spot(m, f), pair_sem, (m, f), ha=partner)

    for f in range(2):
        pair_copy(jnp.int32(0), f, True).start()
    for f in range(2):
        for m in range(1, min(3, chips)):
            same_copy(jnp.int32(m), f).start()

    def peers(src, dst, sems):
        return [
            send_to(src, dst.at[d - 1], sems, (d - 1,), wa=lax.rem(me + d, n))
            for d in range(1, n)
        ]

    small, small_two = peers(sqs, lsq, ssem), peers(sq2, lsq2, s2sem)

    def prepare(g):
        @pl.loop(0, 2 * rows // 16)
        def _(i):
            at = pl.ds(pl.multiple_of(i * 16, 16), 16)
            x = tok[g, at, :].astype(F32)
            scaled[at, :] = (x * jnp.broadcast_to(gain_ref[...].astype(F32).reshape(1, -1), x.shape)).astype(BF16)
            sqp[at, :] = fold_lanes(x * x)

        for e in range(2):
            sqs[pl.ds(g * 2 + e, 1), :] = lane_sums(sqp[pl.ds(e * rows, rows), :])[:1]

    def tables(g):
        for e in range(2):
            for part in range(2):
                m, f = member(g, part, chips)
                allowed = allowed_mask(seg_ref[(mirror(chip, m, chips) * 2 + e) * 2 + f], hrows)
                at = jnp.sum(jnp.where(allowed, 1.0, 0.0), axis=1, keepdims=True) - 1.0
                lanes = lax.broadcasted_iota(jnp.int32, (hrows, WINDOW), 1)
                pick = jnp.where(lanes == at.astype(jnp.int32), 1.0, 0.0)
                cs[g * 2 + e, part * hrows : (part + 1) * hrows, :] = jnp.dot(
                    pick, rope_ref[...], precision=lax.Precision.HIGHEST,
                    preferred_element_type=F32,
                )

    def code_copies(land, steps, sems, step_sems, j, peer):
        return (
            send_to(land, land, sems, (j,), wa=peer),
            send_to(steps, steps, step_sems, (j,), wa=peer),
        )

    def handle(pos, peer, part, land, steps, sems, step_sems, j):
        copies = code_copies(land, steps, sems, step_sems, j, peer)

        @pl.when(pos == 0)
        def _():
            encode(part[...], land, steps, rows)

        @pl.when(pos > 0)
        def _():
            for copy in copies:
                copy.wait_recv()

        @pl.when((pos > 0) & (pos < last))
        def _():
            encode(decode(land, steps, rows) + part[...], land, steps, rows)

        @pl.when(pos < last)
        def _():
            for copy in copies:
                copy.start()

        @pl.when(pos == last)
        def _():
            part[...] = decode(land, steps, rows) + part[...]

    def reduce_step(s, pos, peer, e, q_land, k_land, steps, sems, step_sems):
        j = s - SKEW * pos

        @pl.when((j >= 0) & (j < count))
        def _():
            g, u = lax.div(j, units), lax.rem(j, units)

            @pl.when(u == 0)
            def _():
                handle(
                    pos, peer, parts.at[j], k_land.at[g], steps.at[j], sems, step_sems, j
                )

            @pl.when(u > 0)
            def _():
                jq = g * tiles + u - 1
                part = parts.at[j, pl.ds(e * rows, rows)]
                handle(pos, peer, part, q_land.at[jq], steps.at[j], sems, step_sems, j)

    def front_step(s):
        g, u = lax.div(s, units), lax.rem(s, units)

        @pl.when(s < count)
        def _():
            @pl.when(u == 0)
            def _():
                @pl.when(g == 0)
                def _():
                    own_copy.wait()

                for part in range(2):
                    pair_copy(*member(g, part, chips), False).wait_recv()
                prepare(g)

                @pl.when(g == chips - 1)
                def _():
                    for copy in small:
                        copy.start()

            for v in range(units):

                @pl.when(s == v)
                def _():
                    for copy in w_copies(v):
                        copy.wait()

            parts[s] = jnp.dot(scaled[...], w[u], preferred_element_type=F32)

        @pl.when(s == count)
        def _():
            for c in range(n_wo):
                wo_copy(c).start()

        reduce_step(s, me, right, 1, qr, kr, er, rsem, resem)
        reduce_step(s, last - me, left, 0, ql, kl, el, lsem, lesem)

        @pl.when((s < count) & (u == 1))
        def _():
            tables(g)

        @pl.when((u == max(0, units - FORWARD)) & (g + 1 < chips))
        def _():
            @pl.when(g + 3 < chips)
            def _():
                for f in range(2):
                    same_copy(g + 3, f).start()

            for part in range(2):
                m, f = member(g + 1, part, chips)
                same_copy(m, f).wait_recv()
                pair_copy(m, f, False).start()

    def drain(j, pos, peer, q_land, k_land, steps, sems, step_sems):
        g, u = lax.div(j, units), lax.rem(j, units)

        @pl.when((pos < last) & (u == 0))
        def _():
            for copy in code_copies(k_land.at[g], steps.at[j], sems, step_sems, j, peer):
                copy.wait_send()

        @pl.when((pos < last) & (u > 0))
        def _():
            jq = g * tiles + u - 1
            for copy in code_copies(q_land.at[jq], steps.at[j], sems, step_sems, j, peer):
                copy.wait_send()

    def group(p):
        return jnp.where(
            p == chips - 1, 0, jnp.where(p == 0, 1, jnp.where(p == 1, chips - 1, p))
        )

    def row_scale(k):
        return column(lax.rsqrt(sqs[pl.ds(k, 1), :] / all_width + EPS))

    def rotated(x, turn):
        return x * turn[:, :HD] + pltpu.roll(x, HD // 2, 1) * turn[:, HD:]

    def first_row(g, part, e):
        m, f = member(g, part, chips)
        half = (mirror(chip, m, chips) * 2 + e) * 2 + f
        return half, pl.multiple_of(half * hrows, hrows)

    def settle():
        for m in range(chips):
            for f in range(2):
                pair_copy(jnp.int32(m), f, False).wait_send()
                if m:
                    same_copy(jnp.int32(m), f).wait_send()
        for m in range(1, chips):
            pl.semaphore_signal(
                free_sem, inc=1,
                device_id={"ha": mirror(chip, jnp.int32(m), chips) * 2 + core},
                device_id_type=pl.DeviceIdType.MESH,
            )
        for copy in small:
            copy.wait()
        total = sqs[...]
        for d in range(n - 1):
            total = total + lsq[d]
        sqs[...] = total

        @pl.when(is_end)
        def _():
            zero = jnp.zeros((WINDOW, HD), BF16)
            keys[pl.ds(0, WINDOW), :] = zero
            values[pl.ds(0, WINDOW), :] = zero

            @pl.loop(0, chips)
            def _(g):
                for e in range(2):
                    scale = row_scale(g * 2 + e)
                    block = parts.at[g * units, pl.ds(e * rows, rows)]
                    plain = (block[:, :HD] * scale).astype(BF16).astype(F32)
                    turned = rotated(plain, cs[g * 2 + e]).astype(BF16)
                    value = (block[:, HD:] * scale).astype(BF16)
                    for part in range(2):
                        _, row = first_row(g, part, e)
                        at = pl.ds(pl.multiple_of(WINDOW + row, hrows), hrows)
                        cut = slice(part * hrows, (part + 1) * hrows)
                        keys[at, :] = turned[cut]
                        values[at, :] = value[cut]

    def attend(j):
        p, t = lax.div(j, tiles), lax.rem(j, tiles)
        g = group(p)

        @pl.when(t == 0)
        def _():
            for part in range(2):
                half, _ = first_row(g, part, end_row)
                ones = jnp.where(allowed_mask(seg_ref[half], hrows), 1.0, 0.0)
                mask[part, pl.ds(0, hrows), :] = ones
                mask[part, pl.ds(hrows, hrows), :] = ones
            qscale[...] = jnp.broadcast_to(row_scale(g * 2 + end_row), (rows, HD))

        for part in range(2):
            _, row = first_row(g, part, end_row)
            at = pl.ds(row, window)
            cut = slice(part * hrows, (part + 1) * hrows)
            to = pl.ds(pl.multiple_of(end_row * rows + part * hrows, hrows), hrows)
            turn = cs[g * 2 + end_row, cut, :]
            query = jnp.concatenate(
                [
                    rotated(
                        parts[g * units + 1 + t, to, x * HD : (x + 1) * HD] * qscale[cut, :], turn
                    )
                    for x in range(TILE // HD)
                ],
                axis=0,
            ).astype(BF16)
            allowed = mask[part] > 0.5
            scores = lax.dot_general(
                query, keys[at, :], (((1,), (1,)), ((), ())), preferred_element_type=F32
            ) * HD ** (-0.5)
            scores = jnp.where(allowed, scores, -1e30)
            peak = jnp.max(scores, axis=1, keepdims=True)
            expo = jnp.where(allowed, jnp.exp(scores - peak), 0.0)
            weights = (expo / jnp.sum(expo, axis=1, keepdims=True)).astype(BF16)
            out = jnp.dot(weights, values[at, :], preferred_element_type=F32).astype(BF16)
            for x in range(TILE // HD):
                head[p, t, to, x * HD : (x + 1) * HD] = out[x * hrows : (x + 1) * hrows]

    def spread_copy(j, e, peer, sems):
        ref = head.at[lax.div(j, tiles), lax.rem(j, tiles), pl.ds(e * rows, rows)]
        return send_to(ref, ref, sems, (j,), wa=peer)

    def spread_step(s, pos, peer, e, sems):
        j = s - SPREAD_SKEW * pos

        @pl.when((j >= 0) & (j < n_chunk))
        def _():
            copy = spread_copy(j, e, peer, sems)

            @pl.when(pos > 0)
            def _():
                copy.wait_recv()

            @pl.when(pos < last)
            def _():
                copy.start()

    def swap_copy(v):
        return send_to(
            acc.at[lax.rem(v, RING), theirs], got.at[lax.rem(v, DEEP)], psem, (v,), ha=partner
        )

    def stage(v, part):
        p, k = lax.div(v, wides), lax.rem(v, wides)
        at = pl.ds(pl.multiple_of(k * WIDE, WIDE), WIDE)
        return tok.at[p, pl.ds(rows + part * hrows, hrows), at]

    def land(v, part):
        p, k = lax.div(v, wides), lax.rem(v, wides)
        at = pl.ds(pl.multiple_of(k * WIDE, WIDE), WIDE)
        return tok.at[p, pl.ds(part * hrows, hrows), at]

    def peer_copy(v, part):
        g = group(lax.div(v, wides))
        m, _ = member(g, part, chips)
        if relay and part == 1:
            m = jnp.where(g == chips - 1, 1 + core, m)
        return send_to(
            stage(v, part), land(v, part), xsem, (v, part), ha=mirror(chip, m, chips) * 2 + core
        )

    def project(v):
        p, k = lax.div(v, wides), lax.rem(v, wides)

        @pl.when(v == 0)
        def _():
            for c in range(n_wo):
                wo_copy(c).wait()

        @pl.when(v >= RING)
        def _():
            swap_copy(v - RING).wait_send()

        block = jnp.concatenate([head[p, t] for t in range(tiles)], axis=1)
        for y in range(WIDE // TILE):
            c = k * (WIDE // TILE) + y
            deep = pl.ds(pl.multiple_of(lax.rem(c, fold) * cols, cols), cols)
            acc[lax.rem(v, RING), :, y * TILE : (y + 1) * TILE] = jnp.dot(
                block, w[lax.div(c, fold), deep, :], preferred_element_type=F32
            )

        @pl.when(v >= DEEP)
        def _():
            pl.semaphore_wait(credit_sem, 1)

        swap_copy(v).start()

    def combine(v):
        p, k = lax.div(v, wides), lax.rem(v, wides)
        swap_copy(v).wait_recv()
        both = acc[lax.rem(v, RING), mine, :] + got[lax.rem(v, DEEP)]

        @pl.when(v + DEEP < n_unit)
        def _():
            pl.semaphore_signal(
                credit_sem, inc=1, device_id={"ha": partner},
                device_id_type=pl.DeviceIdType.MESH,
            )

        @pl.when(v == 0)
        def _():
            pl.semaphore_wait(free_sem, chips - 1)

        @pl.when(p < chips - 1)
        def _():
            for part in range(2):
                extra = stage(v, part)
                extra[...] = both[part * hrows : (part + 1) * hrows].astype(BF16)
                if relay:
                    through = wides + k

                    @pl.when((group(p) == chips - 2) & (part == 1 - core))
                    def _():
                        peer_copy(through, 1).wait_recv()
                        here = both[part * hrows : (part + 1) * hrows]
                        extra[...] = (here + land(through, 1)[...].astype(F32)).astype(BF16)

                peer_copy(v, part).start()

        @pl.when(p == chips - 1)
        def _():
            own[k] = both

    @pl.loop(0, start + lag + n_unit + 1)
    def _(s):
        @pl.when(s < count + SKEW * last)
        def _():
            front_step(s)

        @pl.when(s == start)
        def _():
            settle()

        r = s - start

        @pl.when(r >= 0)
        def _():
            @pl.when(is_end & (r < n_chunk))
            def _():
                attend(r)

            spread_step(r, me, right, 0, srsem)
            spread_step(r, last - me, left, 1, slsem)

        v = r - lag

        @pl.when((v >= 0) & (v < n_unit))
        def _():
            project(v)

        @pl.when(v >= 1)
        def _():
            combine(v - 1)

    @pl.loop(0, wides)
    def _(k):
        halves = [own[k, pl.ds(f * hrows, hrows), :] for f in range(2)]
        for p in range(chips - 1):
            g, v = order[p], p * wides + k
            for part in range(2):
                if relay and g == chips - 1 and part == 1:
                    continue
                peer_copy(v, part).wait_recv()
                f = part if g == chips - 1 else (g - 1) % 2
                halves[f] = halves[f] + land(v, part)[...].astype(F32)
        total = jnp.concatenate(halves, axis=0)
        at = pl.ds(pl.multiple_of(k * WIDE, WIDE), WIDE)
        sum_ref[:, at] = total
        wide = (tok_ref[:, at].astype(F32) + total).astype(BF16).astype(F32)
        square = fold_lanes(wide * wide)

        @pl.when(k == 0)
        def _():
            sqp[pl.ds(0, rows), :] = square

        @pl.when(k > 0)
        def _():
            sqp[pl.ds(0, rows), :] = sqp[pl.ds(0, rows), :] + square

    sq2[...] = lane_sums(sqp[pl.ds(0, rows), :])
    for copy in small_two:
        copy.start()

    @pl.loop(0, count)
    def _(j):
        drain(j, me, right, qr, kr, er, rsem, resem)
        drain(j, last - me, left, ql, kl, el, lsem, lesem)

    @pl.loop(0, n_chunk)
    def _(j):
        @pl.when(me < last)
        def _():
            spread_copy(j, 0, right, srsem).wait_send()

        @pl.when(me > 0)
        def _():
            spread_copy(j, 1, left, slsem).wait_send()

    @pl.loop(0, n_unit - wides)
    def _(v):
        for part in range(2):
            peer_copy(v, part).wait_send()

    for v in range(n_unit - RING, n_unit):
        swap_copy(jnp.int32(v)).wait_send()
    for copy in small_two:
        copy.wait()
    total = sq2[...]
    for d in range(n - 1):
        total = total + lsq2[d]
    scale_ref[...] = jnp.broadcast_to(
        column(lax.rsqrt(total[:1] / all_width + EPS)), scale_ref.shape
    )


def layer(tokens, gain, w_query, w_key, w_value, seg_rows, rope, w_out, n, n_ha):
    rows, width = tokens.shape
    cols = w_query.shape[1]
    chips, tiles, wides = n_ha // 2, cols // TILE, width // WIDE
    units = tiles + 1
    count = chips * units
    n_chunk, n_unit = chips * tiles, chips * wides
    vmem, any_ = pl.BlockSpec(memory_space=pltpu.VMEM), pl.BlockSpec(memory_space=pl.ANY)
    dma, reg = pltpu.SemaphoreType.DMA, pltpu.SemaphoreType.REGULAR
    i16 = jnp.int16
    return pl.pallas_call(
        functools.partial(
            layer_kernel, n, chips, rows, tiles, wides, n_ha // KVH, width * n
        ),
        out_shape=(
            jax.ShapeDtypeStruct((rows, width), F32),
            jax.ShapeDtypeStruct((rows, 128), F32),
        ),
        in_specs=[any_, vmem, any_, any_, any_, vmem, vmem, vmem, any_],
        out_specs=(vmem, vmem),
        scratch_shapes=[
            pltpu.VMEM((chips, 2 * rows, width), BF16),
            pltpu.VMEM((2 * rows, width), BF16),
            pltpu.VMEM((units, width, TILE), BF16),
            pltpu.VMEM((count, 2 * rows, TILE), F32),
            pltpu.VMEM((chips * tiles, rows, TILE), i16),
            pltpu.VMEM((chips * tiles, rows, TILE), i16),
            pltpu.VMEM((chips, 2 * rows, TILE), i16),
            pltpu.VMEM((chips, 2 * rows, TILE), i16),
            pltpu.VMEM((count, 4, rows), F32),
            pltpu.VMEM((count, 4, rows), F32),
            pltpu.VMEM((n_ha, rows, 2 * HD), F32),
            pltpu.VMEM((2 * rows, 128), F32),
            pltpu.VMEM((n_ha, rows), F32),
            pltpu.VMEM((n - 1, n_ha, rows), F32),
            pltpu.VMEM((WINDOW + n_ha * rows, HD), BF16),
            pltpu.VMEM((WINDOW + n_ha * rows, HD), BF16),
            pltpu.VMEM((2, rows, WINDOW + rows // 2), F32),
            pltpu.VMEM((rows, HD), F32),
            pltpu.VMEM((chips, tiles, 2 * rows, TILE), BF16),
            pltpu.VMEM((RING, 2 * rows, WIDE), F32),
            pltpu.VMEM((DEEP, rows, WIDE), F32),
            pltpu.VMEM((wides, rows, WIDE), F32),
            pltpu.VMEM((8, rows), F32),
            pltpu.VMEM((n - 1, 8, rows), F32),
            dma((units + 1,)),
            dma,
            dma((2, chips, 2)),
            dma((2, chips, 2)),
            dma((2, count)),
            dma((2, count)),
            dma((2, count)),
            dma((2, count)),
            dma((2, n - 1)),
            dma((wides * (WIDE // TILE),)),
            dma((2, n_chunk)),
            dma((2, n_chunk)),
            dma((2, n_unit)),
            dma((2, n_unit - wides, 2)),
            dma((2, n - 1)),
            reg,
            reg,
        ],
        compiler_params=pltpu.CompilerParams(
            collective_id=0, has_side_effects=True, vmem_limit_bytes=63 << 20
        ),
    )(tokens, gain, w_query, w_key, w_value, seg_rows, rope, tokens, w_out)


def on_device(tokens, gain_attn, w_query, w_key, w_value, w_out, gain_ffn, segment_ids):
    rows, width = tokens.shape
    n_wa = lax.axis_size("wa")
    n_ha = lax.axis_size("ha")
    padded = jnp.pad(segment_ids, (WINDOW, 0), constant_values=-1).astype(F32)
    half = rows // 2
    seg_rows = jnp.stack(
        [padded[None, k * half : (k + 1) * half + WINDOW] for k in range(2 * n_ha)]
    )
    attended, scale_two = layer(
        tokens, gain_attn, w_query, w_key, w_value, seg_rows, rope_rows(),
        w_out, n_wa, n_ha,
    )
    residual_out = (tokens.astype(F32) + attended).astype(BF16)
    ffn_input = (
        residual_out.astype(F32) * scale_two[:, :1] * gain_ffn.astype(F32)
    ).astype(BF16)
    return (residual_out, ffn_input)


def solution(mesh):
    in_specs = (
        P("ha", "wa"),
        P("wa"),
        P("wa", "ha"),
        P("wa", None),
        P("wa", None),
        P("ha", "wa"),
        P("wa"),
        P(),
    )
    out_specs = (P("ha", "wa"), P("ha", "wa"))
    return jax.shard_map(
        on_device, mesh=mesh, in_specs=in_specs, out_specs=out_specs, check_vma=False
    )
```

```python
import functools

import jax
import jax.numpy as jnp
from jax import lax
from jax.experimental import pallas as pl
from jax.experimental.pallas import tpu as pltpu
from jax.sharding import PartitionSpec as P

KVH = 8
HD = 128
WINDOW = 256
EPS = 1e-05
TILE = 256
WIDE = 512
SKEW = 4
SPREAD_SKEW = 3
LEVELS = 32766.0
FORWARD = 3
RING = 4
DEEP = 8
F32 = jnp.float32
BF16 = jnp.bfloat16


def rope_rows():
    half = HD // 2
    inverse = 500000.0 ** (-(jnp.arange(half, dtype=F32) * 2.0 / HD))
    angle = jnp.arange(WINDOW, dtype=F32)[:, None] * inverse[None, :]
    cosine, sine = jnp.cos(angle), jnp.sin(angle)
    return jnp.concatenate([cosine, cosine, -sine, sine], axis=1)


def mirror(a, m, size):
    total, bit = 0, 1
    while bit < size:
        total = total + lax.rem(lax.div(a, bit) + lax.div(m, bit), 2) * bit
        bit *= 2
    return total


def member(g, sub, chips):
    edge = (g == 0) | (g == chips - 1)
    low = lax.div(g - 1, 2) * 2 + 1
    return jnp.where(edge, g, low + sub), jnp.where(edge, sub, lax.rem(g - 1, 2))


def place(m, f, chips):
    edge = (m == 0) | (m == chips - 1)
    low = lax.div(m - 1, 2) * 2 + 1
    return jnp.where(edge, m, low + f), jnp.where(edge, f, lax.rem(m - 1, 2))


def send_to(src, dst, sems, at, **peer):
    return pltpu.make_async_remote_copy(
        src_ref=src,
        dst_ref=dst,
        send_sem=sems.at[(0,) + at],
        recv_sem=sems.at[(1,) + at],
        device_id=peer,
        device_id_type=pl.DeviceIdType.MESH,
    )


def greet(n, chips, me, chip, core):
    barrier = pltpu.get_barrier_semaphore()

    def signal(**peer):
        pl.semaphore_signal(
            barrier, inc=1, device_id=peer, device_id_type=pl.DeviceIdType.MESH
        )

    for d in range(1, n):
        signal(wa=lax.rem(me + d, n))
    for m in range(1, chips):
        signal(ha=mirror(chip, jnp.int32(m), chips) * 2 + core)
    signal(ha=chip * 2 + 1 - core)
    pl.semaphore_wait(barrier, n + chips - 1)


def column(row):
    r = row.shape[1]
    a = lax.broadcasted_iota(jnp.int32, (r, r), 0)
    b = lax.broadcasted_iota(jnp.int32, (r, r), 1)
    return jnp.sum(jnp.where(a == b, jnp.broadcast_to(row, (r, r)), 0.0), axis=1, keepdims=True)


def as_row(col):
    r = col.shape[0]
    a = lax.broadcasted_iota(jnp.int32, (r, r), 0)
    b = lax.broadcasted_iota(jnp.int32, (r, r), 1)
    return jnp.sum(jnp.where(a == b, jnp.broadcast_to(col, (r, r)), 0.0), axis=0, keepdims=True)


def encode(x, code, steps, rows):
    for i in range(x.shape[0] // rows):
        for y in range(TILE // HD):
            part = x[i * rows : (i + 1) * rows, y * HD : (y + 1) * HD]
            top = jnp.maximum(jnp.max(jnp.abs(part), axis=1, keepdims=True), 1e-30)
            whole = jnp.round(part * (LEVELS / top)).astype(jnp.int32)
            code[i * rows : (i + 1) * rows, y * HD : (y + 1) * HD] = whole.astype(jnp.int16)
            k = i * 2 + y
            steps[k : k + 1, :] = as_row(top * (1.0 / LEVELS))


def decode(code, steps, rows):
    blocks = []
    for i in range(code.shape[0] // rows):
        line = []
        for y in range(TILE // HD):
            part = code[i * rows : (i + 1) * rows, y * HD : (y + 1) * HD]
            k = i * 2 + y
            line.append(part.astype(jnp.int32).astype(F32) * column(steps[k : k + 1, :]))
        blocks.append(jnp.concatenate(line, axis=1))
    return jnp.concatenate(blocks, axis=0)


def lane_sums(block):
    ones = jnp.ones((8, block.shape[1]), F32)
    return lax.dot_general(
        ones, block, (((1,), (1,)), ((), ())), precision=lax.Precision.HIGHEST,
        preferred_element_type=F32,
    )


def fold_lanes(x):
    total = x[:, :128]
    for g in range(1, x.shape[1] // 128):
        total = total + x[:, g * 128 : (g + 1) * 128]
    return total


def allowed_mask(seg_row, rows):
    keys = seg_row.shape[1]
    q_seg = column(seg_row[:, keys - rows :])
    q_at = lax.broadcasted_iota(jnp.int32, (rows, keys), 0) + (keys - rows)
    k_at = lax.broadcasted_iota(jnp.int32, (rows, keys), 1)
    return (q_seg == seg_row) & (k_at <= q_at)


def plan(n, chips, tiles, wides):
    units = tiles + 1
    start = (chips - 1) * units + SKEW * (n - 1)
    lag = max(0, tiles - wides) * chips + tiles - 1 + SPREAD_SKEW * (n - 1)
    return start, lag


def layer_kernel(
    n, chips, rows, tiles, wides, per_head, all_width,
    tok_hbm, gain_ref, wq_hbm, wk_hbm, wv_hbm, seg_ref, rope_ref, tok_ref, wo_hbm,
    sum_ref, scale_ref,
    tok, scaled, w, parts, qr, ql, kr, kl, er, el, cs, sqp, sqs, lsq,
    keys, values, mask, qscale, head, acc, got, own, sq2, lsq2,
    wsem, tsem, same_sem, pair_sem, rsem, lsem, resem, lesem, ssem,
    osem, srsem, slsem, psem, xsem, s2sem, free_sem, credit_sem,
):
    me, ha = lax.axis_index("wa"), lax.axis_index("ha")
    core, chip = lax.rem(ha, 2), lax.div(ha, 2)
    last = n - 1
    units = tiles + 1
    count = chips * units
    n_chunk, n_unit = chips * tiles, chips * wides
    start, lag = plan(n, chips, tiles, wides)
    hrows = rows // 2
    window = WINDOW + hrows
    cols = tiles * TILE
    fold = w.shape[1] // cols
    own_at = pl.multiple_of(core * rows, rows)
    kv_at = pl.multiple_of(lax.div(ha, per_head) * HD, HD)
    partner = chip * 2 + 1 - core
    mine = pl.ds(own_at, rows)
    theirs = pl.ds(pl.multiple_of((1 - core) * rows, rows), rows)
    right, left = jnp.minimum(me + 1, last), jnp.maximum(me - 1, 0)
    end_row = jnp.where(me == last, 1, 0)
    is_end = (me == 0) | (me == last)
    relay = chips == 4
    order = ([1, chips - 1] + list(range(2, chips - 1)))[: chips - 1] + [0]

    def w_copies(u):
        if u == 0:
            return [
                pltpu.make_async_copy(
                    wk_hbm.at[:, pl.ds(kv_at, HD)], w.at[0, :, pl.ds(0, HD)], wsem.at[0]
                ),
                pltpu.make_async_copy(
                    wv_hbm.at[:, pl.ds(kv_at, HD)], w.at[0, :, pl.ds(HD, HD)], wsem.at[1]
                ),
            ]
        return [
            pltpu.make_async_copy(
                wq_hbm.at[:, pl.ds((u - 1) * TILE, TILE)], w.at[u], wsem.at[u + 1]
            )
        ]

    def wo_copy(c):
        return pltpu.make_async_copy(
            wo_hbm.at[:, pl.ds(c * TILE, TILE)],
            w.at[c // fold, pl.ds((c % fold) * cols, cols)],
            osem.at[c],
        )

    n_wo = wides * (WIDE // TILE)

    own_copy = pltpu.make_async_copy(tok_hbm, tok.at[0, mine], tsem)
    own_copy.start()
    for u in range(units):
        for copy in w_copies(u):
            copy.start()
    greet(n, chips, me, chip, core)

    def half_rows(f):
        return pl.ds(pl.multiple_of(f * hrows, hrows), hrows)

    def spot(m, f):
        g, part = place(m, f, chips)
        return tok.at[g, pl.ds(pl.multiple_of(own_at + part * hrows, hrows), hrows)]

    def same_copy(m, f):
        return send_to(
            tok_hbm.at[half_rows(f)], spot(m, f), same_sem, (m, f),
            ha=mirror(chip, m, chips) * 2 + core,
        )

    def pair_copy(m, f, first):
        src = tok_hbm.at[half_rows(f)] if first else spot(m, f)
        return send_to(src, spot(m, f), pair_sem, (m, f), ha=partner)

    for f in range(2):
        pair_copy(jnp.int32(0), f, True).start()
    for f in range(2):
        for m in range(1, min(3, chips)):
            same_copy(jnp.int32(m), f).start()

    def peers(src, dst, sems):
        return [
            send_to(src, dst.at[d - 1], sems, (d - 1,), wa=lax.rem(me + d, n))
            for d in range(1, n)
        ]

    small, small_two = peers(sqs, lsq, ssem), peers(sq2, lsq2, s2sem)

    def prepare(g):
        @pl.loop(0, 2 * rows // 16)
        def _(i):
            at = pl.ds(pl.multiple_of(i * 16, 16), 16)
            x = tok[g, at, :].astype(F32)
            scaled[at, :] = (x * jnp.broadcast_to(gain_ref[...].astype(F32).reshape(1, -1), x.shape)).astype(BF16)
            sqp[at, :] = fold_lanes(x * x)

        for e in range(2):
            sqs[pl.ds(g * 2 + e, 1), :] = lane_sums(sqp[pl.ds(e * rows, rows), :])[:1]

    def tables(g):
        for e in range(2):
            for part in range(2):
                m, f = member(g, part, chips)
                allowed = allowed_mask(seg_ref[(mirror(chip, m, chips) * 2 + e) * 2 + f], hrows)
                at = jnp.sum(jnp.where(allowed, 1.0, 0.0), axis=1, keepdims=True) - 1.0
                lanes = lax.broadcasted_iota(jnp.int32, (hrows, WINDOW), 1)
                pick = jnp.where(lanes == at.astype(jnp.int32), 1.0, 0.0)
                cs[g * 2 + e, part * hrows : (part + 1) * hrows, :] = jnp.dot(
                    pick, rope_ref[...], precision=lax.Precision.HIGHEST,
                    preferred_element_type=F32,
                )

    def code_copies(land, steps, sems, step_sems, j, peer):
        return (
            send_to(land, land, sems, (j,), wa=peer),
            send_to(steps, steps, step_sems, (j,), wa=peer),
        )

    def handle(pos, peer, part, land, steps, sems, step_sems, j):
        copies = code_copies(land, steps, sems, step_sems, j, peer)

        @pl.when(pos == 0)
        def _():
            encode(part[...], land, steps, rows)

        @pl.when(pos > 0)
        def _():
            for copy in copies:
                copy.wait_recv()

        @pl.when((pos > 0) & (pos < last))
        def _():
            encode(decode(land, steps, rows) + part[...], land, steps, rows)

        @pl.when(pos < last)
        def _():
            for copy in copies:
                copy.start()

        @pl.when(pos == last)
        def _():
            part[...] = decode(land, steps, rows) + part[...]

    def reduce_step(s, pos, peer, e, q_land, k_land, steps, sems, step_sems):
        j = s - SKEW * pos

        @pl.when((j >= 0) & (j < count))
        def _():
            g, u = lax.div(j, units), lax.rem(j, units)

            @pl.when(u == 0)
            def _():
                handle(
                    pos, peer, parts.at[j], k_land.at[g], steps.at[j], sems, step_sems, j
                )

            @pl.when(u > 0)
            def _():
                jq = g * tiles + u - 1
                part = parts.at[j, pl.ds(e * rows, rows)]
                handle(pos, peer, part, q_land.at[jq], steps.at[j], sems, step_sems, j)

    def front_step(s):
        g, u = lax.div(s, units), lax.rem(s, units)

        @pl.when(s < count)
        def _():
            @pl.when(u == 0)
            def _():
                @pl.when(g == 0)
                def _():
                    own_copy.wait()

                for part in range(2):
                    pair_copy(*member(g, part, chips), False).wait_recv()
                prepare(g)

                @pl.when(g == chips - 1)
                def _():
                    for copy in small:
                        copy.start()

            for v in range(units):

                @pl.when(s == v)
                def _():
                    for copy in w_copies(v):
                        copy.wait()

            parts[s] = jnp.dot(scaled[...], w[u], preferred_element_type=F32)

        @pl.when(s == count)
        def _():
            for c in range(n_wo):
                wo_copy(c).start()

        reduce_step(s, me, right, 1, qr, kr, er, rsem, resem)
        reduce_step(s, last - me, left, 0, ql, kl, el, lsem, lesem)

        @pl.when((s < count) & (u == 1))
        def _():
            tables(g)

        @pl.when((u == max(0, units - FORWARD)) & (g + 1 < chips))
        def _():
            @pl.when(g + 3 < chips)
            def _():
                for f in range(2):
                    same_copy(g + 3, f).start()

            for part in range(2):
                m, f = member(g + 1, part, chips)
                same_copy(m, f).wait_recv()
                pair_copy(m, f, False).start()

    def drain(j, pos, peer, q_land, k_land, steps, sems, step_sems):
        g, u = lax.div(j, units), lax.rem(j, units)

        @pl.when((pos < last) & (u == 0))
        def _():
            for copy in code_copies(k_land.at[g], steps.at[j], sems, step_sems, j, peer):
                copy.wait_send()

        @pl.when((pos < last) & (u > 0))
        def _():
            jq = g * tiles + u - 1
            for copy in code_copies(q_land.at[jq], steps.at[j], sems, step_sems, j, peer):
                copy.wait_send()

    def group(p):
        return jnp.where(
            p == chips - 1, 0, jnp.where(p == 0, 1, jnp.where(p == 1, chips - 1, p))
        )

    def row_scale(k):
        return column(lax.rsqrt(sqs[pl.ds(k, 1), :] / all_width + EPS))

    def rotated(x, turn):
        return x * turn[:, :HD] + pltpu.roll(x, HD // 2, 1) * turn[:, HD:]

    def first_row(g, part, e):
        m, f = member(g, part, chips)
        half = (mirror(chip, m, chips) * 2 + e) * 2 + f
        return half, pl.multiple_of(half * hrows, hrows)

    def settle():
        for m in range(chips):
            for f in range(2):
                pair_copy(jnp.int32(m), f, False).wait_send()
                if m:
                    same_copy(jnp.int32(m), f).wait_send()
        for m in range(1, chips):
            pl.semaphore_signal(
                free_sem, inc=1,
                device_id={"ha": mirror(chip, jnp.int32(m), chips) * 2 + core},
                device_id_type=pl.DeviceIdType.MESH,
            )
        for copy in small:
            copy.wait()
        total = sqs[...]
        for d in range(n - 1):
            total = total + lsq[d]
        sqs[...] = total

        @pl.when(is_end)
        def _():
            zero = jnp.zeros((WINDOW, HD), BF16)
            keys[pl.ds(0, WINDOW), :] = zero
            values[pl.ds(0, WINDOW), :] = zero

            @pl.loop(0, chips)
            def _(g):
                for e in range(2):
                    scale = row_scale(g * 2 + e)
                    block = parts.at[g * units, pl.ds(e * rows, rows)]
                    plain = (block[:, :HD] * scale).astype(BF16).astype(F32)
                    turned = rotated(plain, cs[g * 2 + e]).astype(BF16)
                    value = (block[:, HD:] * scale).astype(BF16)
                    for part in range(2):
                        _, row = first_row(g, part, e)
                        at = pl.ds(pl.multiple_of(WINDOW + row, hrows), hrows)
                        cut = slice(part * hrows, (part + 1) * hrows)
                        keys[at, :] = turned[cut]
                        values[at, :] = value[cut]

    def attend(j):
        p, t = lax.div(j, tiles), lax.rem(j, tiles)
        g = group(p)

        @pl.when(t == 0)
        def _():
            for part in range(2):
                half, _ = first_row(g, part, end_row)
                ones = jnp.where(allowed_mask(seg_ref[half], hrows), 1.0, 0.0)
                mask[part, pl.ds(0, hrows), :] = ones
                mask[part, pl.ds(hrows, hrows), :] = ones
            qscale[...] = jnp.broadcast_to(row_scale(g * 2 + end_row), (rows, HD))

        for part in range(2):
            _, row = first_row(g, part, end_row)
            at = pl.ds(row, window)
            cut = slice(part * hrows, (part + 1) * hrows)
            to = pl.ds(pl.multiple_of(end_row * rows + part * hrows, hrows), hrows)
            turn = cs[g * 2 + end_row, cut, :]
            query = jnp.concatenate(
                [
                    rotated(
                        parts[g * units + 1 + t, to, x * HD : (x + 1) * HD] * qscale[cut, :], turn
                    )
                    for x in range(TILE // HD)
                ],
                axis=0,
            ).astype(BF16)
            allowed = mask[part] > 0.5
            scores = lax.dot_general(
                query, keys[at, :], (((1,), (1,)), ((), ())), preferred_element_type=F32
            ) * HD ** (-0.5)
            scores = jnp.where(allowed, scores, -1e30)
            peak = jnp.max(scores, axis=1, keepdims=True)
            expo = jnp.where(allowed, jnp.exp(scores - peak), 0.0)
            weights = (expo / jnp.sum(expo, axis=1, keepdims=True)).astype(BF16)
            out = jnp.dot(weights, values[at, :], preferred_element_type=F32).astype(BF16)
            for x in range(TILE // HD):
                head[p, t, to, x * HD : (x + 1) * HD] = out[x * hrows : (x + 1) * hrows]

    def spread_copy(j, e, peer, sems):
        ref = head.at[lax.div(j, tiles), lax.rem(j, tiles), pl.ds(e * rows, rows)]
        return send_to(ref, ref, sems, (j,), wa=peer)

    def spread_step(s, pos, peer, e, sems):
        j = s - SPREAD_SKEW * pos

        @pl.when((j >= 0) & (j < n_chunk))
        def _():
            copy = spread_copy(j, e, peer, sems)

            @pl.when(pos > 0)
            def _():
                copy.wait_recv()

            @pl.when(pos < last)
            def _():
                copy.start()

    def swap_copy(v):
        return send_to(
            acc.at[lax.rem(v, RING), theirs], got.at[lax.rem(v, DEEP)], psem, (v,), ha=partner
        )

    def stage(v, part):
        p, k = lax.div(v, wides), lax.rem(v, wides)
        at = pl.ds(pl.multiple_of(k * WIDE, WIDE), WIDE)
        return tok.at[p, pl.ds(rows + part * hrows, hrows), at]

    def land(v, part):
        p, k = lax.div(v, wides), lax.rem(v, wides)
        at = pl.ds(pl.multiple_of(k * WIDE, WIDE), WIDE)
        return tok.at[p, pl.ds(part * hrows, hrows), at]

    def peer_copy(v, part):
        g = group(lax.div(v, wides))
        m, _ = member(g, part, chips)
        if relay and part == 1:
            m = jnp.where(g == chips - 1, 1 + core, m)
        return send_to(
            stage(v, part), land(v, part), xsem, (v, part), ha=mirror(chip, m, chips) * 2 + core
        )

    def project(v):
        p, k = lax.div(v, wides), lax.rem(v, wides)

        @pl.when(v == 0)
        def _():
            for c in range(n_wo):
                wo_copy(c).wait()

        @pl.when(v >= RING)
        def _():
            swap_copy(v - RING).wait_send()

        block = jnp.concatenate([head[p, t] for t in range(tiles)], axis=1)
        for y in range(WIDE // TILE):
            c = k * (WIDE // TILE) + y
            deep = pl.ds(pl.multiple_of(lax.rem(c, fold) * cols, cols), cols)
            acc[lax.rem(v, RING), :, y * TILE : (y + 1) * TILE] = jnp.dot(
                block, w[lax.div(c, fold), deep, :], preferred_element_type=F32
            )

        @pl.when(v >= DEEP)
        def _():
            pl.semaphore_wait(credit_sem, 1)

        swap_copy(v).start()

    def combine(v):
        p, k = lax.div(v, wides), lax.rem(v, wides)
        swap_copy(v).wait_recv()
        both = acc[lax.rem(v, RING), mine, :] + got[lax.rem(v, DEEP)]

        @pl.when(v + DEEP < n_unit)
        def _():
            pl.semaphore_signal(
                credit_sem, inc=1, device_id={"ha": partner},
                device_id_type=pl.DeviceIdType.MESH,
            )

        @pl.when(v == 0)
        def _():
            pl.semaphore_wait(free_sem, chips - 1)

        @pl.when(p < chips - 1)
        def _():
            for part in range(2):
                extra = stage(v, part)
                extra[...] = both[part * hrows : (part + 1) * hrows].astype(BF16)
                if relay:
                    through = wides + k

                    @pl.when((group(p) == chips - 2) & (part == 1 - core))
                    def _():
                        peer_copy(through, 1).wait_recv()
                        here = both[part * hrows : (part + 1) * hrows]
                        extra[...] = (here + land(through, 1)[...].astype(F32)).astype(BF16)

                peer_copy(v, part).start()

        @pl.when(p == chips - 1)
        def _():
            own[k] = both

    @pl.loop(0, start + lag + n_unit + 1)
    def _(s):
        @pl.when(s < count + SKEW * last)
        def _():
            front_step(s)

        @pl.when(s == start)
        def _():
            settle()

        r = s - start

        @pl.when(r >= 0)
        def _():
            @pl.when(is_end & (r < n_chunk))
            def _():
                attend(r)

            spread_step(r, me, right, 0, srsem)
            spread_step(r, last - me, left, 1, slsem)

        v = r - lag

        @pl.when((v >= 0) & (v < n_unit))
        def _():
            project(v)

        @pl.when(v >= 1)
        def _():
            combine(v - 1)

    @pl.loop(0, wides)
    def _(k):
        halves = [own[k, pl.ds(f * hrows, hrows), :] for f in range(2)]
        for p in range(chips - 1):
            g, v = order[p], p * wides + k
            for part in range(2):
                if relay and g == chips - 1 and part == 1:
                    continue
                peer_copy(v, part).wait_recv()
                f = part if g == chips - 1 else (g - 1) % 2
                halves[f] = halves[f] + land(v, part)[...].astype(F32)
        total = jnp.concatenate(halves, axis=0)
        at = pl.ds(pl.multiple_of(k * WIDE, WIDE), WIDE)
        sum_ref[:, at] = total
        wide = (tok_ref[:, at].astype(F32) + total).astype(BF16).astype(F32)
        square = fold_lanes(wide * wide)

        @pl.when(k == 0)
        def _():
            sqp[pl.ds(0, rows), :] = square

        @pl.when(k > 0)
        def _():
            sqp[pl.ds(0, rows), :] = sqp[pl.ds(0, rows), :] + square

    sq2[...] = lane_sums(sqp[pl.ds(0, rows), :])
    for copy in small_two:
        copy.start()

    @pl.loop(0, count)
    def _(j):
        drain(j, me, right, qr, kr, er, rsem, resem)
        drain(j, last - me, left, ql, kl, el, lsem, lesem)

    @pl.loop(0, n_chunk)
    def _(j):
        @pl.when(me < last)
        def _():
            spread_copy(j, 0, right, srsem).wait_send()

        @pl.when(me > 0)
        def _():
            spread_copy(j, 1, left, slsem).wait_send()

    @pl.loop(0, n_unit - wides)
    def _(v):
        for part in range(2):
            peer_copy(v, part).wait_send()

    for v in range(n_unit - RING, n_unit):
        swap_copy(jnp.int32(v)).wait_send()
    for copy in small_two:
        copy.wait()
    total = sq2[...]
    for d in range(n - 1):
        total = total + lsq2[d]
    scale_ref[...] = jnp.broadcast_to(
        column(lax.rsqrt(total[:1] / all_width + EPS)), scale_ref.shape
    )


def layer(tokens, gain, w_query, w_key, w_value, seg_rows, rope, w_out, n, n_ha):
    rows, width = tokens.shape
    cols = w_query.shape[1]
    chips, tiles, wides = n_ha // 2, cols // TILE, width // WIDE
    units = tiles + 1
    count = chips * units
    n_chunk, n_unit = chips * tiles, chips * wides
    vmem, any_ = pl.BlockSpec(memory_space=pltpu.VMEM), pl.BlockSpec(memory_space=pl.ANY)
    dma, reg = pltpu.SemaphoreType.DMA, pltpu.SemaphoreType.REGULAR
    i16 = jnp.int16
    return pl.pallas_call(
        functools.partial(
            layer_kernel, n, chips, rows, tiles, wides, n_ha // KVH, width * n
        ),
        out_shape=(
            jax.ShapeDtypeStruct((rows, width), F32),
            jax.ShapeDtypeStruct((rows, 128), F32),
        ),
        in_specs=[any_, vmem, any_, any_, any_, vmem, vmem, vmem, any_],
        out_specs=(vmem, vmem),
        scratch_shapes=[
            pltpu.VMEM((chips, 2 * rows, width), BF16),
            pltpu.VMEM((2 * rows, width), BF16),
            pltpu.VMEM((units, width, TILE), BF16),
            pltpu.VMEM((count, 2 * rows, TILE), F32),
            pltpu.VMEM((chips * tiles, rows, TILE), i16),
            pltpu.VMEM((chips * tiles, rows, TILE), i16),
            pltpu.VMEM((chips, 2 * rows, TILE), i16),
            pltpu.VMEM((chips, 2 * rows, TILE), i16),
            pltpu.VMEM((count, 4, rows), F32),
            pltpu.VMEM((count, 4, rows), F32),
            pltpu.VMEM((n_ha, rows, 2 * HD), F32),
            pltpu.VMEM((2 * rows, 128), F32),
            pltpu.VMEM((n_ha, rows), F32),
            pltpu.VMEM((n - 1, n_ha, rows), F32),
            pltpu.VMEM((WINDOW + n_ha * rows, HD), BF16),
            pltpu.VMEM((WINDOW + n_ha * rows, HD), BF16),
            pltpu.VMEM((2, rows, WINDOW + rows // 2), F32),
            pltpu.VMEM((rows, HD), F32),
            pltpu.VMEM((chips, tiles, 2 * rows, TILE), BF16),
            pltpu.VMEM((RING, 2 * rows, WIDE), F32),
            pltpu.VMEM((DEEP, rows, WIDE), F32),
            pltpu.VMEM((wides, rows, WIDE), F32),
            pltpu.VMEM((8, rows), F32),
            pltpu.VMEM((n - 1, 8, rows), F32),
            dma((units + 1,)),
            dma,
            dma((2, chips, 2)),
            dma((2, chips, 2)),
            dma((2, count)),
            dma((2, count)),
            dma((2, count)),
            dma((2, count)),
            dma((2, n - 1)),
            dma((wides * (WIDE // TILE),)),
            dma((2, n_chunk)),
            dma((2, n_chunk)),
            dma((2, n_unit)),
            dma((2, n_unit - wides, 2)),
            dma((2, n - 1)),
            reg,
            reg,
        ],
        compiler_params=pltpu.CompilerParams(
            collective_id=0, has_side_effects=True, vmem_limit_bytes=63 << 20
        ),
    )(tokens, gain, w_query, w_key, w_value, seg_rows, rope, tokens, w_out)


def on_device(tokens, gain_attn, w_query, w_key, w_value, w_out, gain_ffn, segment_ids):
    rows, width = tokens.shape
    n_wa = lax.axis_size("wa")
    n_ha = lax.axis_size("ha")
    padded = jnp.pad(segment_ids, (WINDOW, 0), constant_values=-1).astype(F32)
    half = rows // 2
    seg_rows = jnp.stack(
        [padded[None, k * half : (k + 1) * half + WINDOW] for k in range(2 * n_ha)]
    )
    attended, scale_two = layer(
        tokens, gain_attn, w_query, w_key, w_value, seg_rows, rope_rows(),
        w_out, n_wa, n_ha,
    )
    residual_out = (tokens.astype(F32) + attended).astype(BF16)
    ffn_input = (
        residual_out.astype(F32) * scale_two[:, :1] * gain_ffn.astype(F32)
    ).astype(BF16)
    return (residual_out, ffn_input)


def solution(mesh):
    in_specs = (
        P("ha", "wa"),
        P("wa"),
        P("wa", "ha"),
        P("wa", None),
        P("wa", None),
        P("ha", "wa"),
        P("wa"),
        P(),
    )
    out_specs = (P("ha", "wa"), P("ha", "wa"))
    return jax.shard_map(
        on_device, mesh=mesh, in_specs=in_specs, out_specs=out_specs, check_vma=False
    )
```

```python
import functools

import jax
import jax.numpy as jnp
from jax import lax
from jax.experimental import pallas as pl
from jax.experimental.pallas import tpu as pltpu
from jax.sharding import PartitionSpec as P

KVH = 8
HD = 128
WINDOW = 256
EPS = 1e-05
TILE = 256
WIDE = 512
SKEW = 4
SPREAD_SKEW = 3
LEVELS = 32766.0
FORWARD = 3
RING = 4
DEEP = 8
F32 = jnp.float32
BF16 = jnp.bfloat16


def rope_rows():
    half = HD // 2
    inverse = 500000.0 ** (-(jnp.arange(half, dtype=F32) * 2.0 / HD))
    angle = jnp.arange(WINDOW, dtype=F32)[:, None] * inverse[None, :]
    cosine, sine = jnp.cos(angle), jnp.sin(angle)
    return jnp.concatenate([cosine, cosine, -sine, sine], axis=1)


def mirror(a, m, size):
    total, bit = 0, 1
    while bit < size:
        total = total + lax.rem(lax.div(a, bit) + lax.div(m, bit), 2) * bit
        bit *= 2
    return total


def member(g, sub, chips):
    edge = (g == 0) | (g == chips - 1)
    low = lax.div(g - 1, 2) * 2 + 1
    return jnp.where(edge, g, low + sub), jnp.where(edge, sub, lax.rem(g - 1, 2))


def place(m, f, chips):
    edge = (m == 0) | (m == chips - 1)
    low = lax.div(m - 1, 2) * 2 + 1
    return jnp.where(edge, m, low + f), jnp.where(edge, f, lax.rem(m - 1, 2))


def send_to(src, dst, sems, at, **peer):
    return pltpu.make_async_remote_copy(
        src_ref=src,
        dst_ref=dst,
        send_sem=sems.at[(0,) + at],
        recv_sem=sems.at[(1,) + at],
        device_id=peer,
        device_id_type=pl.DeviceIdType.MESH,
    )


def greet(n, chips, me, chip, core):
    barrier = pltpu.get_barrier_semaphore()

    def signal(**peer):
        pl.semaphore_signal(
            barrier, inc=1, device_id=peer, device_id_type=pl.DeviceIdType.MESH
        )

    for d in range(1, n):
        signal(wa=lax.rem(me + d, n))
    for m in range(1, chips):
        signal(ha=mirror(chip, jnp.int32(m), chips) * 2 + core)
    signal(ha=chip * 2 + 1 - core)
    pl.semaphore_wait(barrier, n + chips - 1)


def column(row):
    r = row.shape[1]
    a = lax.broadcasted_iota(jnp.int32, (r, r), 0)
    b = lax.broadcasted_iota(jnp.int32, (r, r), 1)
    return jnp.sum(jnp.where(a == b, jnp.broadcast_to(row, (r, r)), 0.0), axis=1, keepdims=True)


def as_row(col):
    r = col.shape[0]
    a = lax.broadcasted_iota(jnp.int32, (r, r), 0)
    b = lax.broadcasted_iota(jnp.int32, (r, r), 1)
    return jnp.sum(jnp.where(a == b, jnp.broadcast_to(col, (r, r)), 0.0), axis=0, keepdims=True)


def encode(x, code, steps, rows):
    for i in range(x.shape[0] // rows):
        for y in range(TILE // HD):
            part = x[i * rows : (i + 1) * rows, y * HD : (y + 1) * HD]
            top = jnp.maximum(jnp.max(jnp.abs(part), axis=1, keepdims=True), 1e-30)
            whole = jnp.round(part * (LEVELS / top)).astype(jnp.int32)
            code[i * rows : (i + 1) * rows, y * HD : (y + 1) * HD] = whole.astype(jnp.int16)
            k = i * 2 + y
            steps[k : k + 1, :] = as_row(top * (1.0 / LEVELS))


def decode(code, steps, rows):
    blocks = []
    for i in range(code.shape[0] // rows):
        line = []
        for y in range(TILE // HD):
            part = code[i * rows : (i + 1) * rows, y * HD : (y + 1) * HD]
            k = i * 2 + y
            line.append(part.astype(jnp.int32).astype(F32) * column(steps[k : k + 1, :]))
        blocks.append(jnp.concatenate(line, axis=1))
    return jnp.concatenate(blocks, axis=0)


def lane_sums(block):
    ones = jnp.ones((8, block.shape[1]), F32)
    return lax.dot_general(
        ones, block, (((1,), (1,)), ((), ())), precision=lax.Precision.HIGHEST,
        preferred_element_type=F32,
    )


def fold_lanes(x):
    total = x[:, :128]
    for g in range(1, x.shape[1] // 128):
        total = total + x[:, g * 128 : (g + 1) * 128]
    return total


def allowed_mask(seg_row, rows):
    keys = seg_row.shape[1]
    q_seg = column(seg_row[:, keys - rows :])
    q_at = lax.broadcasted_iota(jnp.int32, (rows, keys), 0) + (keys - rows)
    k_at = lax.broadcasted_iota(jnp.int32, (rows, keys), 1)
    return (q_seg == seg_row) & (k_at <= q_at)


def plan(n, chips, tiles, wides):
    units = tiles + 1
    start = (chips - 1) * units + SKEW * (n - 1)
    lag = max(0, tiles - wides) * chips + tiles - 1 + SPREAD_SKEW * (n - 1)
    return start, lag


def layer_kernel(
    n, chips, rows, tiles, wides, per_head, all_width,
    tok_hbm, gain_ref, wq_hbm, wk_hbm, wv_hbm, seg_ref, rope_ref, tok_ref, wo_hbm,
    sum_ref, scale_ref,
    tok, scaled, w, parts, qr, ql, kr, kl, er, el, cs, sqp, sqs, lsq,
    keys, values, mask, qscale, head, acc, got, own, sq2, lsq2,
    wsem, tsem, same_sem, pair_sem, rsem, lsem, resem, lesem, ssem,
    osem, srsem, slsem, psem, xsem, s2sem, free_sem, credit_sem,
):
    me, ha = lax.axis_index("wa"), lax.axis_index("ha")
    core, chip = lax.rem(ha, 2), lax.div(ha, 2)
    last = n - 1
    units = tiles + 1
    count = chips * units
    n_chunk, n_unit = chips * tiles, chips * wides
    start, lag = plan(n, chips, tiles, wides)
    hrows = rows // 2
    window = WINDOW + hrows
    cols = tiles * TILE
    fold = w.shape[1] // cols
    own_at = pl.multiple_of(core * rows, rows)
    kv_at = pl.multiple_of(lax.div(ha, per_head) * HD, HD)
    partner = chip * 2 + 1 - core
    mine = pl.ds(own_at, rows)
    theirs = pl.ds(pl.multiple_of((1 - core) * rows, rows), rows)
    right, left = jnp.minimum(me + 1, last), jnp.maximum(me - 1, 0)
    end_row = jnp.where(me == last, 1, 0)
    is_end = (me == 0) | (me == last)
    relay = chips == 4
    order = ([1, chips - 1] + list(range(2, chips - 1)))[: chips - 1] + [0]

    def w_copies(u):
        if u == 0:
            return [
                pltpu.make_async_copy(
                    wk_hbm.at[:, pl.ds(kv_at, HD)], w.at[0, :, pl.ds(0, HD)], wsem.at[0]
                ),
                pltpu.make_async_copy(
                    wv_hbm.at[:, pl.ds(kv_at, HD)], w.at[0, :, pl.ds(HD, HD)], wsem.at[1]
                ),
            ]
        return [
            pltpu.make_async_copy(
                wq_hbm.at[:, pl.ds((u - 1) * TILE, TILE)], w.at[u], wsem.at[u + 1]
            )
        ]

    def wo_copy(c):
        return pltpu.make_async_copy(
            wo_hbm.at[:, pl.ds(c * TILE, TILE)],
            w.at[c // fold, pl.ds((c % fold) * cols, cols)],
            osem.at[c],
        )

    n_wo = wides * (WIDE // TILE)

    own_copy = pltpu.make_async_copy(tok_hbm, tok.at[0, mine], tsem)
    own_copy.start()
    for u in range(units):
        for copy in w_copies(u):
            copy.start()
    greet(n, chips, me, chip, core)

    def half_rows(f):
        return pl.ds(pl.multiple_of(f * hrows, hrows), hrows)

    def spot(m, f):
        g, part = place(m, f, chips)
        return tok.at[g, pl.ds(pl.multiple_of(own_at + part * hrows, hrows), hrows)]

    def same_copy(m, f):
        return send_to(
            tok_hbm.at[half_rows(f)], spot(m, f), same_sem, (m, f),
            ha=mirror(chip, m, chips) * 2 + core,
        )

    def pair_copy(m, f, first):
        src = tok_hbm.at[half_rows(f)] if first else spot(m, f)
        return send_to(src, spot(m, f), pair_sem, (m, f), ha=partner)

    for f in range(2):
        pair_copy(jnp.int32(0), f, True).start()
    for f in range(2):
        for m in range(1, min(3, chips)):
            same_copy(jnp.int32(m), f).start()

    def peers(src, dst, sems):
        return [
            send_to(src, dst.at[d - 1], sems, (d - 1,), wa=lax.rem(me + d, n))
            for d in range(1, n)
        ]

    small, small_two = peers(sqs, lsq, ssem), peers(sq2, lsq2, s2sem)

    def prepare(g):
        @pl.loop(0, 2 * rows // 16)
        def _(i):
            at = pl.ds(pl.multiple_of(i * 16, 16), 16)
            x = tok[g, at, :].astype(F32)
            scaled[at, :] = (x * jnp.broadcast_to(gain_ref[...].astype(F32).reshape(1, -1), x.shape)).astype(BF16)
            sqp[at, :] = fold_lanes(x * x)

        for e in range(2):
            sqs[pl.ds(g * 2 + e, 1), :] = lane_sums(sqp[pl.ds(e * rows, rows), :])[:1]

    def tables(g):
        for e in range(2):
            for part in range(2):
                m, f = member(g, part, chips)
                allowed = allowed_mask(seg_ref[(mirror(chip, m, chips) * 2 + e) * 2 + f], hrows)
                at = jnp.sum(jnp.where(allowed, 1.0, 0.0), axis=1, keepdims=True) - 1.0
                lanes = lax.broadcasted_iota(jnp.int32, (hrows, WINDOW), 1)
                pick = jnp.where(lanes == at.astype(jnp.int32), 1.0, 0.0)
                cs[g * 2 + e, part * hrows : (part + 1) * hrows, :] = jnp.dot(
                    pick, rope_ref[...], precision=lax.Precision.HIGHEST,
                    preferred_element_type=F32,
                )

    def code_copies(land, steps, sems, step_sems, j, peer):
        return (
            send_to(land, land, sems, (j,), wa=peer),
            send_to(steps, steps, step_sems, (j,), wa=peer),
        )

    def handle(pos, peer, part, land, steps, sems, step_sems, j):
        copies = code_copies(land, steps, sems, step_sems, j, peer)

        @pl.when(pos == 0)
        def _():
            encode(part[...], land, steps, rows)

        @pl.when(pos > 0)
        def _():
            for copy in copies:
                copy.wait_recv()

        @pl.when((pos > 0) & (pos < last))
        def _():
            encode(decode(land, steps, rows) + part[...], land, steps, rows)

        @pl.when(pos < last)
        def _():
            for copy in copies:
                copy.start()

        @pl.when(pos == last)
        def _():
            part[...] = decode(land, steps, rows) + part[...]

    def reduce_step(s, pos, peer, e, q_land, k_land, steps, sems, step_sems):
        j = s - SKEW * pos

        @pl.when((j >= 0) & (j < count))
        def _():
            g, u = lax.div(j, units), lax.rem(j, units)

            @pl.when(u == 0)
            def _():
                handle(
                    pos, peer, parts.at[j], k_land.at[g], steps.at[j], sems, step_sems, j
                )

            @pl.when(u > 0)
            def _():
                jq = g * tiles + u - 1
                part = parts.at[j, pl.ds(e * rows, rows)]
                handle(pos, peer, part, q_land.at[jq], steps.at[j], sems, step_sems, j)

    def front_step(s):
        g, u = lax.div(s, units), lax.rem(s, units)

        @pl.when(s < count)
        def _():
            @pl.when(u == 0)
            def _():
                @pl.when(g == 0)
                def _():
                    own_copy.wait()

                for part in range(2):
                    pair_copy(*member(g, part, chips), False).wait_recv()
                prepare(g)

                @pl.when(g == chips - 1)
                def _():
                    for copy in small:
                        copy.start()

            for v in range(units):

                @pl.when(s == v)
                def _():
                    for copy in w_copies(v):
                        copy.wait()

            parts[s] = jnp.dot(scaled[...], w[u], preferred_element_type=F32)

        @pl.when(s == count)
        def _():
            for c in range(n_wo):
                wo_copy(c).start()

        reduce_step(s, me, right, 1, qr, kr, er, rsem, resem)
        reduce_step(s, last - me, left, 0, ql, kl, el, lsem, lesem)

        @pl.when((s < count) & (u == 1))
        def _():
            tables(g)

        @pl.when((u == max(0, units - FORWARD)) & (g + 1 < chips))
        def _():
            @pl.when(g + 3 < chips)
            def _():
                for f in range(2):
                    same_copy(g + 3, f).start()

            for part in range(2):
                m, f = member(g + 1, part, chips)
                same_copy(m, f).wait_recv()
                pair_copy(m, f, False).start()

    def drain(j, pos, peer, q_land, k_land, steps, sems, step_sems):
        g, u = lax.div(j, units), lax.rem(j, units)

        @pl.when((pos < last) & (u == 0))
        def _():
            for copy in code_copies(k_land.at[g], steps.at[j], sems, step_sems, j, peer):
                copy.wait_send()

        @pl.when((pos < last) & (u > 0))
        def _():
            jq = g * tiles + u - 1
            for copy in code_copies(q_land.at[jq], steps.at[j], sems, step_sems, j, peer):
                copy.wait_send()

    def group(p):
        return jnp.where(
            p == chips - 1, 0, jnp.where(p == 0, 1, jnp.where(p == 1, chips - 1, p))
        )

    def row_scale(k):
        return column(lax.rsqrt(sqs[pl.ds(k, 1), :] / all_width + EPS))

    def rotated(x, turn):
        return x * turn[:, :HD] + pltpu.roll(x, HD // 2, 1) * turn[:, HD:]

    def first_row(g, part, e):
        m, f = member(g, part, chips)
        half = (mirror(chip, m, chips) * 2 + e) * 2 + f
        return half, pl.multiple_of(half * hrows, hrows)

    def settle():
        for m in range(chips):
            for f in range(2):
                pair_copy(jnp.int32(m), f, False).wait_send()
                if m:
                    same_copy(jnp.int32(m), f).wait_send()
        for m in range(1, chips):
            pl.semaphore_signal(
                free_sem, inc=1,
                device_id={"ha": mirror(chip, jnp.int32(m), chips) * 2 + core},
                device_id_type=pl.DeviceIdType.MESH,
            )
        for copy in small:
            copy.wait()
        total = sqs[...]
        for d in range(n - 1):
            total = total + lsq[d]
        sqs[...] = total

        @pl.when(is_end)
        def _():
            zero = jnp.zeros((WINDOW, HD), BF16)
            keys[pl.ds(0, WINDOW), :] = zero
            values[pl.ds(0, WINDOW), :] = zero

            @pl.loop(0, chips)
            def _(g):
                for e in range(2):
                    scale = row_scale(g * 2 + e)
                    block = parts.at[g * units, pl.ds(e * rows, rows)]
                    plain = (block[:, :HD] * scale).astype(BF16).astype(F32)
                    turned = rotated(plain, cs[g * 2 + e]).astype(BF16)
                    value = (block[:, HD:] * scale).astype(BF16)
                    for part in range(2):
                        _, row = first_row(g, part, e)
                        at = pl.ds(pl.multiple_of(WINDOW + row, hrows), hrows)
                        cut = slice(part * hrows, (part + 1) * hrows)
                        keys[at, :] = turned[cut]
                        values[at, :] = value[cut]

    def attend(j):
        p, t = lax.div(j, tiles), lax.rem(j, tiles)
        g = group(p)

        @pl.when(t == 0)
        def _():
            for part in range(2):
                half, _ = first_row(g, part, end_row)
                ones = jnp.where(allowed_mask(seg_ref[half], hrows), 1.0, 0.0)
                mask[part, pl.ds(0, hrows), :] = ones
                mask[part, pl.ds(hrows, hrows), :] = ones
            qscale[...] = jnp.broadcast_to(row_scale(g * 2 + end_row), (rows, HD))

        for part in range(2):
            _, row = first_row(g, part, end_row)
            at = pl.ds(row, window)
            cut = slice(part * hrows, (part + 1) * hrows)
            to = pl.ds(pl.multiple_of(end_row * rows + part * hrows, hrows), hrows)
            turn = cs[g * 2 + end_row, cut, :]
            query = jnp.concatenate(
                [
                    rotated(
                        parts[g * units + 1 + t, to, x * HD : (x + 1) * HD] * qscale[cut, :], turn
                    )
                    for x in range(TILE // HD)
                ],
                axis=0,
            ).astype(BF16)
            allowed = mask[part] > 0.5
            scores = lax.dot_general(
                query, keys[at, :], (((1,), (1,)), ((), ())), preferred_element_type=F32
            ) * HD ** (-0.5)
            scores = jnp.where(allowed, scores, -1e30)
            peak = jnp.max(scores, axis=1, keepdims=True)
            expo = jnp.where(allowed, jnp.exp(scores - peak), 0.0)
            weights = (expo / jnp.sum(expo, axis=1, keepdims=True)).astype(BF16)
            out = jnp.dot(weights, values[at, :], preferred_element_type=F32).astype(BF16)
            for x in range(TILE // HD):
                head[p, t, to, x * HD : (x + 1) * HD] = out[x * hrows : (x + 1) * hrows]

    def spread_copy(j, e, peer, sems):
        ref = head.at[lax.div(j, tiles), lax.rem(j, tiles), pl.ds(e * rows, rows)]
        return send_to(ref, ref, sems, (j,), wa=peer)

    def spread_step(s, pos, peer, e, sems):
        j = s - SPREAD_SKEW * pos

        @pl.when((j >= 0) & (j < n_chunk))
        def _():
            copy = spread_copy(j, e, peer, sems)

            @pl.when(pos > 0)
            def _():
                copy.wait_recv()

            @pl.when(pos < last)
            def _():
                copy.start()

    def swap_copy(v):
        return send_to(
            acc.at[lax.rem(v, RING), theirs], got.at[lax.rem(v, DEEP)], psem, (v,), ha=partner
        )

    def stage(v, part):
        p, k = lax.div(v, wides), lax.rem(v, wides)
        at = pl.ds(pl.multiple_of(k * WIDE, WIDE), WIDE)
        return tok.at[p, pl.ds(rows + part * hrows, hrows), at]

    def land(v, part):
        p, k = lax.div(v, wides), lax.rem(v, wides)
        at = pl.ds(pl.multiple_of(k * WIDE, WIDE), WIDE)
        return tok.at[p, pl.ds(part * hrows, hrows), at]

    def peer_copy(v, part):
        g = group(lax.div(v, wides))
        m, _ = member(g, part, chips)
        if relay and part == 1:
            m = jnp.where(g == chips - 1, 1 + core, m)
        return send_to(
            stage(v, part), land(v, part), xsem, (v, part), ha=mirror(chip, m, chips) * 2 + core
        )

    def project(v):
        p, k = lax.div(v, wides), lax.rem(v, wides)

        @pl.when(v == 0)
        def _():
            for c in range(n_wo):
                wo_copy(c).wait()

        @pl.when(v >= RING)
        def _():
            swap_copy(v - RING).wait_send()

        block = jnp.concatenate([head[p, t] for t in range(tiles)], axis=1)
        for y in range(WIDE // TILE):
            c = k * (WIDE // TILE) + y
            deep = pl.ds(pl.multiple_of(lax.rem(c, fold) * cols, cols), cols)
            acc[lax.rem(v, RING), :, y * TILE : (y + 1) * TILE] = jnp.dot(
                block, w[lax.div(c, fold), deep, :], preferred_element_type=F32
            )

        @pl.when(v >= DEEP)
        def _():
            pl.semaphore_wait(credit_sem, 1)

        swap_copy(v).start()

    def combine(v):
        p, k = lax.div(v, wides), lax.rem(v, wides)
        swap_copy(v).wait_recv()
        both = acc[lax.rem(v, RING), mine, :] + got[lax.rem(v, DEEP)]

        @pl.when(v + DEEP < n_unit)
        def _():
            pl.semaphore_signal(
                credit_sem, inc=1, device_id={"ha": partner},
                device_id_type=pl.DeviceIdType.MESH,
            )

        @pl.when(v == 0)
        def _():
            pl.semaphore_wait(free_sem, chips - 1)

        @pl.when(p < chips - 1)
        def _():
            for part in range(2):
                extra = stage(v, part)
                extra[...] = both[part * hrows : (part + 1) * hrows].astype(BF16)
                if relay:
                    through = wides + k

                    @pl.when((group(p) == chips - 2) & (part == 1 - core))
                    def _():
                        peer_copy(through, 1).wait_recv()
                        here = both[part * hrows : (part + 1) * hrows]
                        extra[...] = (here + land(through, 1)[...].astype(F32)).astype(BF16)

                peer_copy(v, part).start()

        @pl.when(p == chips - 1)
        def _():
            own[k] = both

    def spread_drain(j):
        @pl.when(me < last)
        def _():
            spread_copy(j, 0, right, srsem).wait_send()

        @pl.when(me > 0)
        def _():
            spread_copy(j, 1, left, slsem).wait_send()

    drained, spent = min(count, lag + n_unit + 1), min(n_chunk, n_unit)

    @pl.loop(0, start + lag + n_unit + 1)
    def _(s):
        @pl.when(s < count + SKEW * last)
        def _():
            front_step(s)

        @pl.when(s == start)
        def _():
            settle()

        r = s - start

        @pl.when(r >= 0)
        def _():
            @pl.when(is_end & (r < n_chunk))
            def _():
                attend(r)

            spread_step(r, me, right, 0, srsem)
            spread_step(r, last - me, left, 1, slsem)

        v = r - lag

        @pl.when((r >= 0) & (r < drained))
        def _():
            drain(r, me, right, qr, kr, er, rsem, resem)
            drain(r, last - me, left, ql, kl, el, lsem, lesem)

        @pl.when((v >= 0) & (v < spent))
        def _():
            spread_drain(v)

        @pl.when((v >= 0) & (v < n_unit))
        def _():
            project(v)

        @pl.when(v >= 1)
        def _():
            combine(v - 1)

    @pl.loop(0, wides)
    def _(k):
        halves = [own[k, pl.ds(f * hrows, hrows), :] for f in range(2)]
        for p in range(chips - 1):
            g, v = order[p], p * wides + k
            for part in range(2):
                if relay and g == chips - 1 and part == 1:
                    continue
                peer_copy(v, part).wait_recv()
                f = part if g == chips - 1 else (g - 1) % 2
                halves[f] = halves[f] + land(v, part)[...].astype(F32)
        total = jnp.concatenate(halves, axis=0)
        at = pl.ds(pl.multiple_of(k * WIDE, WIDE), WIDE)
        sum_ref[:, at] = total
        wide = (tok_ref[:, at].astype(F32) + total).astype(BF16).astype(F32)
        square = fold_lanes(wide * wide)

        @pl.when(k == 0)
        def _():
            sqp[pl.ds(0, rows), :] = square

        @pl.when(k > 0)
        def _():
            sqp[pl.ds(0, rows), :] = sqp[pl.ds(0, rows), :] + square

    sq2[...] = lane_sums(sqp[pl.ds(0, rows), :])
    for copy in small_two:
        copy.start()

    @pl.loop(drained, count)
    def _(j):
        drain(j, me, right, qr, kr, er, rsem, resem)
        drain(j, last - me, left, ql, kl, el, lsem, lesem)

    @pl.loop(spent, n_chunk)
    def _(j):
        spread_drain(j)

    @pl.loop(0, n_unit - wides)
    def _(v):
        for part in range(2):
            peer_copy(v, part).wait_send()

    for v in range(n_unit - RING, n_unit):
        swap_copy(jnp.int32(v)).wait_send()
    for copy in small_two:
        copy.wait()
    total = sq2[...]
    for d in range(n - 1):
        total = total + lsq2[d]
    scale_ref[...] = jnp.broadcast_to(
        column(lax.rsqrt(total[:1] / all_width + EPS)), scale_ref.shape
    )


def layer(tokens, gain, w_query, w_key, w_value, seg_rows, rope, w_out, n, n_ha):
    rows, width = tokens.shape
    cols = w_query.shape[1]
    chips, tiles, wides = n_ha // 2, cols // TILE, width // WIDE
    units = tiles + 1
    count = chips * units
    n_chunk, n_unit = chips * tiles, chips * wides
    vmem, any_ = pl.BlockSpec(memory_space=pltpu.VMEM), pl.BlockSpec(memory_space=pl.ANY)
    dma, reg = pltpu.SemaphoreType.DMA, pltpu.SemaphoreType.REGULAR
    i16 = jnp.int16
    return pl.pallas_call(
        functools.partial(
            layer_kernel, n, chips, rows, tiles, wides, n_ha // KVH, width * n
        ),
        out_shape=(
            jax.ShapeDtypeStruct((rows, width), F32),
            jax.ShapeDtypeStruct((rows, 128), F32),
        ),
        in_specs=[any_, vmem, any_, any_, any_, vmem, vmem, vmem, any_],
        out_specs=(vmem, vmem),
        scratch_shapes=[
            pltpu.VMEM((chips, 2 * rows, width), BF16),
            pltpu.VMEM((2 * rows, width), BF16),
            pltpu.VMEM((units, width, TILE), BF16),
            pltpu.VMEM((count, 2 * rows, TILE), F32),
            pltpu.VMEM((chips * tiles, rows, TILE), i16),
            pltpu.VMEM((chips * tiles, rows, TILE), i16),
            pltpu.VMEM((chips, 2 * rows, TILE), i16),
            pltpu.VMEM((chips, 2 * rows, TILE), i16),
            pltpu.VMEM((count, 4, rows), F32),
            pltpu.VMEM((count, 4, rows), F32),
            pltpu.VMEM((n_ha, rows, 2 * HD), F32),
            pltpu.VMEM((2 * rows, 128), F32),
            pltpu.VMEM((n_ha, rows), F32),
            pltpu.VMEM((n - 1, n_ha, rows), F32),
            pltpu.VMEM((WINDOW + n_ha * rows, HD), BF16),
            pltpu.VMEM((WINDOW + n_ha * rows, HD), BF16),
            pltpu.VMEM((2, rows, WINDOW + rows // 2), F32),
            pltpu.VMEM((rows, HD), F32),
            pltpu.VMEM((chips, tiles, 2 * rows, TILE), BF16),
            pltpu.VMEM((RING, 2 * rows, WIDE), F32),
            pltpu.VMEM((DEEP, rows, WIDE), F32),
            pltpu.VMEM((wides, rows, WIDE), F32),
            pltpu.VMEM((8, rows), F32),
            pltpu.VMEM((n - 1, 8, rows), F32),
            dma((units + 1,)),
            dma,
            dma((2, chips, 2)),
            dma((2, chips, 2)),
            dma((2, count)),
            dma((2, count)),
            dma((2, count)),
            dma((2, count)),
            dma((2, n - 1)),
            dma((wides * (WIDE // TILE),)),
            dma((2, n_chunk)),
            dma((2, n_chunk)),
            dma((2, n_unit)),
            dma((2, n_unit - wides, 2)),
            dma((2, n - 1)),
            reg,
            reg,
        ],
        compiler_params=pltpu.CompilerParams(
            collective_id=0, has_side_effects=True, vmem_limit_bytes=63 << 20
        ),
    )(tokens, gain, w_query, w_key, w_value, seg_rows, rope, tokens, w_out)


def on_device(tokens, gain_attn, w_query, w_key, w_value, w_out, gain_ffn, segment_ids):
    rows, width = tokens.shape
    n_wa = lax.axis_size("wa")
    n_ha = lax.axis_size("ha")
    padded = jnp.pad(segment_ids, (WINDOW, 0), constant_values=-1).astype(F32)
    half = rows // 2
    seg_rows = jnp.stack(
        [padded[None, k * half : (k + 1) * half + WINDOW] for k in range(2 * n_ha)]
    )
    attended, scale_two = layer(
        tokens, gain_attn, w_query, w_key, w_value, seg_rows, rope_rows(),
        w_out, n_wa, n_ha,
    )
    residual_out = (tokens.astype(F32) + attended).astype(BF16)
    ffn_input = (
        residual_out.astype(F32) * scale_two[:, :1] * gain_ffn.astype(F32)
    ).astype(BF16)
    return (residual_out, ffn_input)


def solution(mesh):
    in_specs = (
        P("ha", "wa"),
        P("wa"),
        P("wa", "ha"),
        P("wa", None),
        P("wa", None),
        P("ha", "wa"),
        P("wa"),
        P(),
    )
    out_specs = (P("ha", "wa"), P("ha", "wa"))
    return jax.shard_map(
        on_device, mesh=mesh, in_specs=in_specs, out_specs=out_specs, check_vma=False
    )
```
